32 devices in a mesh: sub: 4 (over y, x), row: 8 (over z, core).
Axes of the slice: x: 2, y: 2, z: 4, core: 2. Of those that a mesh axis runs over, the one named last changes fastest.
Arguments:
- inverse: float32 [4, 1024, 12288], P('sub', 'row')
- sources: float32 [4, 16, 12288], P('sub', None, 'row'), may hold values from -6 to 6
- line_history: float32 [4, 32, 1024], P('sub', None, 'row'), may hold values from -6 to 6
- line_dest: int32 [4, 1024], P('sub', 'row'), may hold values from 0 to 3, as said below
- line_port: int32 [4, 1024], P('sub', 'row'), may hold values from 0 to 1023
- line_delay: int32 [4, 1024], P('sub', 'row'), may hold values from 16 to 32
- prev_voltage: float32 [4, 1024], P('sub', 'row'), may hold values from -6 to 6
- flux_start: float32 [4, 1024], P('sub', 'row'), may hold values from -3 to 3
- arrester_gain: float32 [4, 1024], P('sub', 'row'), may hold values from 0.5 to 4
- core_gain: float32 [4, 1024], P('sub', 'row'), may hold values from 0.25 to 2
- arrester_slots: int32 [4, 128], P('sub', 'row'), may hold values from 0 to 127, as said below
- core_slots: int32 [4, 128], P('sub', 'row'), may hold values from 0 to 127, as said below
Outputs:
- voltages: float32 [4, 16, 1024], P('sub', None, 'row')
- final_flux: float32 [4, 1024], P('sub', 'row')
The draws below stay inside these ranges and needn't reach their ends.
Inputs may be any that keep to these rules, and one draw needn't show every extreme that they name: `line_dest`: a record never names its own subnetwork; among the 128 records of one device no subnetwork is named more than 86 times, and in every such block some subnetwork is named exactly 86 times. `arrester_slots`: the 16 entries of one device are distinct slots of that device's 128 ports and share no slot with that device's core entries. `core_slots`: the 16 entries of one device are distinct slots of that device's 128 ports.
All inputs are finite; a program needn't handle non-finite values.
Results may differ from the reference program's by a relative error of at most 0.0003.
Values sent between devices are 32-bit elements; how exact they have to be, the bound alone decides.
A program may use at most 64 MiB of HBM per device.

```python
import math
import jax
import jax.numpy as jnp
from jax import lax

ORDER = 12288
PORT_DEV = 128
LINE_DEV = 128
STEPS = 16
HISTORY = 32
NEWTON = 2
ARREST_DEV = 16
CORE_DEV = 16
SUBNETWORK_COUNT = 4
PORTS = 1024
SLICE = 1536
LINES = 1024
CAPACITY = 86
ARRESTERS = 128
CORES = 128


def line_tables(key):
    base_key = jax.random.fold_in(key, 11)
    row_count = LINES // LINE_DEV
    blocks = SUBNETWORK_COUNT * row_count
    total_options = (SUBNETWORK_COUNT - 1) * CAPACITY

    def one_block(index):
        block_random_key = jax.random.fold_in(base_key, index)
        extra_score_key, forced_pick_key, jitter_key, port_random_key, delay_random_key = jax.random.split(block_random_key, 5)
        owner = index // row_count
        remaining_items = jnp.arange(total_options, dtype=jnp.int32) // CAPACITY
        extra_score = jax.random.randint(extra_score_key, (SUBNETWORK_COUNT - 1,), 0, 3)
        forced_pick = jax.random.randint(forced_pick_key, (), 0, SUBNETWORK_COUNT - 1)
        extra_score = jnp.where(jnp.arange(SUBNETWORK_COUNT - 1, dtype=jnp.int32) == forced_pick, 8, extra_score)
        random_jitter = jax.random.randint(jitter_key, (total_options,), 0, 1024)
        ranking_scores = (extra_score[remaining_items] * 1024 + random_jitter) * 1024 + jnp.arange(total_options, dtype=jnp.int32)
        ignored, chosen = lax.top_k(ranking_scores, LINE_DEV)
        picked = remaining_items[chosen]
        target = picked + (picked >= owner).astype(jnp.int32)
        target_port = jax.random.randint(port_random_key, (LINE_DEV,), 0, PORTS)
        travel = jax.random.randint(delay_random_key, (LINE_DEV,), STEPS, HISTORY + 1)
        return (target.astype(jnp.int32), target_port.astype(jnp.int32), travel.astype(jnp.int32))
    target, target_port, travel = jax.vmap(one_block)(jnp.arange(blocks, dtype=jnp.int32))
    return (target.reshape(SUBNETWORK_COUNT, LINES), target_port.reshape(SUBNETWORK_COUNT, LINES), travel.reshape(SUBNETWORK_COUNT, LINES))


def draw_line_dest(key, part):
    return line_tables(key)[0]


def draw_line_port(key, part):
    return line_tables(key)[1]


def draw_line_delay(key, part):
    return line_tables(key)[2]


def slot_tables(key):
    base_key = jax.random.fold_in(key, 23)
    blocks = SUBNETWORK_COUNT * (PORTS // PORT_DEV)

    def one_block(index):
        ordering = jax.random.permutation(jax.random.fold_in(base_key, index), PORT_DEV).astype(jnp.int32)
        return (ordering[:ARREST_DEV], ordering[ARREST_DEV:ARREST_DEV + CORE_DEV])
    arrest_part, core_part = jax.vmap(one_block)(jnp.arange(blocks, dtype=jnp.int32))
    return (arrest_part.reshape(SUBNETWORK_COUNT, ARRESTERS), core_part.reshape(SUBNETWORK_COUNT, CORES))


def draw_arrester_slots(key, part):
    return slot_tables(key)[0]


def draw_core_slots(key, part):
    return slot_tables(key)[1]


def draw_inverse(key, part):
    base_key = jax.random.fold_in(key, 31)
    key_body, key_diag = jax.random.split(base_key)
    spread = jax.random.normal(key_body, (SUBNETWORK_COUNT, PORTS, ORDER), jnp.float32) * (0.7 / math.sqrt(ORDER))
    diagonal = jnp.exp(jax.random.uniform(key_diag, (SUBNETWORK_COUNT, PORTS), jnp.float32, math.log(0.3), 0.0))
    port_iota = jnp.arange(PORTS, dtype=jnp.int32)
    node_of = port_iota // PORT_DEV * SLICE + port_iota % PORT_DEV
    on_diagonal = node_of[:, None] == jnp.arange(ORDER, dtype=jnp.int32)[None, :]
    return jnp.where(on_diagonal[None, :, :], diagonal[:, :, None], spread)


def level_of(key, dims, cuts, smallest, high):
    factor_of, own = 1.0, jax.random.fold_in(key, 6)
    for axis_at, shards_of in cuts:
        draws = jnp.exp(jax.random.uniform(jax.random.fold_in(own, axis_at), (shards_of,), jnp.float32, smallest / len(cuts), high / len(cuts)))
        factor_of = factor_of * jnp.repeat(draws, dims[axis_at] // shards_of).reshape([-1 if axis == axis_at else 1 for axis in range(len(dims))])
    return factor_of


def gaussian(rng, dims, scale, bound, cuts=(), kind=jnp.bfloat16):
    loudness = level_of(rng, dims, cuts, -0.22, 0.18) if cuts else 1.0
    drawn = jax.random.normal(rng, dims, jnp.float32) * scale * loudness
    return jnp.minimum(jnp.maximum(drawn, -bound), bound).astype(kind)


def setup_inputs(seed: int = 0) -> dict:
    arg_keys = jax.random.split(jax.random.key(seed), 13)
    return {
        "inverse": draw_inverse(jax.random.fold_in(arg_keys[12], 71), 0),
        "sources": gaussian(arg_keys[1], (SUBNETWORK_COUNT, STEPS, ORDER), 1.0, 6.0, ((0, 4), (2, 8)), jnp.float32),
        "line_history": gaussian(arg_keys[2], (SUBNETWORK_COUNT, HISTORY, LINES), 1.0, 6.0, ((0, 4), (2, 8)), jnp.float32),
        "line_dest": draw_line_dest(jax.random.fold_in(arg_keys[12], 71), 0),
        "line_port": draw_line_port(jax.random.fold_in(arg_keys[12], 71), 0),
        "line_delay": draw_line_delay(jax.random.fold_in(arg_keys[12], 71), 0),
        "prev_voltage": gaussian(arg_keys[6], (SUBNETWORK_COUNT, PORTS), 1.0, 6.0, ((0, 4), (1, 8)), jnp.float32),
        "flux_start": gaussian(arg_keys[7], (SUBNETWORK_COUNT, PORTS), 0.5, 3.0, ((0, 4), (1, 8)), jnp.float32),
        "arrester_gain": jnp.clip(jnp.exp(math.log(4.0) - 2.0794415 * jax.random.uniform(arg_keys[8], (SUBNETWORK_COUNT, PORTS), jnp.float32) ** level_of(arg_keys[8], (SUBNETWORK_COUNT, PORTS), ((0, 4), (1, 8)), -0.2, 0.2)), 0.5, 4.0),
        "core_gain": jnp.clip(jnp.exp(math.log(2.0) - 2.0794415 * jax.random.uniform(arg_keys[9], (SUBNETWORK_COUNT, PORTS), jnp.float32) ** level_of(arg_keys[9], (SUBNETWORK_COUNT, PORTS), ((0, 4), (1, 8)), -0.2, 0.2)), 0.25, 2.0),
        "arrester_slots": draw_arrester_slots(jax.random.fold_in(arg_keys[12], 71), 0),
        "core_slots": draw_core_slots(jax.random.fold_in(arg_keys[12], 71), 0),
    }


half_step = 0.25
knee_volts = 1.5
cubic_term = 0.25


def slot_mask(slots, per_block):
    entries = slots.shape[1]
    port_of = (jnp.arange(entries, dtype=jnp.int32) // per_block) * PORT_DEV + slots
    hits = port_of[:, :, None] == jnp.arange(PORTS, dtype=jnp.int32)[None, None, :]
    return jnp.any(hits, axis=1).astype(jnp.float32)


def element_terms(iterate, voltage, flux_now, arrester_mask, arrester_gain, core_mask, core_gain):
    linked = flux_now + half_step * (iterate + voltage)
    ratio = iterate / knee_volts
    current = arrester_mask * arrester_gain * iterate * (1.0 + ratio * ratio) + core_mask * core_gain * (linked + cubic_term * linked * linked * linked)
    slope_now = arrester_mask * arrester_gain * (1.0 + 3.0 * ratio * ratio) + core_mask * core_gain * half_step * (1.0 + 3.0 * cubic_term * linked * linked)
    return current, slope_now


def reference(inverse, sources, line_history, line_dest, line_port, line_delay, prev_voltage, flux_start, arrester_gain, core_gain, arrester_slots, core_slots):
    row_count = PORTS // PORT_DEV
    records = SUBNETWORK_COUNT * LINES
    flat_hist = jnp.transpose(line_history, (1, 0, 2)).reshape(HISTORY, records)
    delays = line_delay.reshape(records)
    lag_index = HISTORY + jnp.arange(STEPS, dtype=jnp.int32)[:, None] - delays[None, :]
    picked = jnp.take_along_axis(flat_hist, lag_index, axis=0)
    segment = (line_dest * PORTS + line_port).reshape(records)
    summed = jax.ops.segment_sum(picked.T, segment, num_segments=SUBNETWORK_COUNT * PORTS)
    history = -jnp.transpose(summed.reshape(SUBNETWORK_COUNT, PORTS, STEPS), (0, 2, 1))
    padded = jnp.pad(history.reshape(SUBNETWORK_COUNT, STEPS, row_count, PORT_DEV), ((0, 0), (0, 0), (0, 0), (0, SLICE - PORT_DEV)))
    injection = sources + padded.reshape(SUBNETWORK_COUNT, STEPS, ORDER)
    linear = jnp.einsum("spn,stn->stp", inverse, injection, precision=lax.Precision.HIGHEST)
    coupling = inverse.reshape(SUBNETWORK_COUNT, PORTS, row_count, SLICE)[:, :, :, :PORT_DEV].reshape(SUBNETWORK_COUNT, PORTS, PORTS)
    self_imp = jnp.diagonal(coupling, axis1=1, axis2=2)
    arrester_mask = slot_mask(arrester_slots, ARREST_DEV)
    core_mask = slot_mask(core_slots, CORE_DEV)

    def advance(carried, linear_now):
        voltage, flux_now = carried
        iterate = voltage
        for newton_pass in range(NEWTON):
            current, slope_now = element_terms(iterate, voltage, flux_now, arrester_mask, arrester_gain, core_mask, core_gain)
            network = linear_now - jnp.einsum("spq,sq->sp", coupling, current, precision=lax.Precision.HIGHEST)
            iterate = iterate - (iterate - network) / (1.0 + self_imp * slope_now)
        return (iterate, flux_now + half_step * (iterate + voltage)), iterate

    (last_voltage, final_flux), stacked = lax.scan(advance, (prev_voltage, flux_start), jnp.transpose(linear, (1, 0, 2)))
    return jnp.transpose(stacked, (1, 0, 2)), final_flux
```

```python
import functools

import jax
import jax.numpy as jnp
from jax import lax
from jax.experimental import pallas as pl
from jax.experimental.pallas import tpu as pltpu
from jax.sharding import PartitionSpec as P

STEPS = 16
HISTORY = 32
NEWTON = 2
CHUNKS = 2
LANES = 128
TAGS = 3

half_step = 0.25
knee_volts = 1.5
cubic_term = 0.25

F32 = jnp.float32
BF16 = jnp.bfloat16
MESH = pl.DeviceIdType.MESH
NN = (((1,), (0,)), ((), ()))
NT = (((1,), (1,)), ((), ()))
HIGHEST = lax.Precision.HIGHEST


def iota(shape, axis):
    return lax.broadcasted_iota(jnp.int32, shape, axis)


def hi_lo(x):
    high = x.astype(BF16)
    return high, (x - high.astype(F32)).astype(BF16)


def stack_hi_lo(x):
    return jnp.concatenate(hi_lo(x), axis=0)


def dot(a, b, dims=NN):
    return lax.dot_general(a, b, dims, preferred_element_type=F32)


def four_terms(r):
    n, m = r.shape[0] // 2, r.shape[1] // 2
    return (r[:n, :m] + r[n:, :m]) + (r[:n, m:] + r[n:, m:])


def kernel(
    subs, rows, ports, slice_len, arrests, cores, n_small,
    inv, src, *refs,
):
    small_hbm, refs = refs[:n_small], refs[n_small:]
    out, refs = refs[0], refs[1:]
    small, refs = refs[:n_small], refs[n_small:]
    (
        m32, m2, mp32, mp2, gath, unit, got_units, elem, fst, x2, wc, fall, vo, cu, acc, hacc,
        small_sem, inv_sem, mp_sem, src_sem, line_send, line_recv, unit_send, unit_recv,
        sub_send, sub_recv, both_send, both_recv, elem_send, elem_recv, fst_send, fst_recv,
    ) = refs
    hist, dest, port, delay, prev, flux, again, cgain, aslots, cslots = small
    s = lax.axis_index("sub")
    me = lax.axis_index("row")
    z, c = me // 2, me % 2
    zn = rows // 2
    partner = z * 2 + (1 - c)
    elems = arrests + cores
    group = LANES // elems
    total = rows * elems
    halves = total // LANES
    width = slice_len // CHUNKS
    peers = subs - 1
    turns = 2 * (zn - 1)

    barrier = pltpu.get_barrier_semaphore()
    for j in range(1, rows):
        pl.semaphore_signal(barrier, inc=1, device_id=(s, lax.rem(me + j, rows)), device_id_type=MESH)
    for j in range(1, subs):
        pl.semaphore_signal(barrier, inc=1, device_id=(lax.rem(s + j, subs), me), device_id_type=MESH)

    small_copies = [
        pltpu.make_async_copy(small_hbm[i], small[i], small_sem.at[i]) for i in range(n_small)
    ]
    for copy in small_copies:
        copy.start()

    def src_copy(k):
        return pltpu.make_async_copy(
            src.at[0, :, pl.ds(k * width, width)], gath.at[k, me], src_sem.at[k]
        )

    for k in range(CHUNKS):
        src_copy(k).start()

    def mp_copy(r):
        return pltpu.make_async_copy(
            inv.at[0, :, pl.ds(r * slice_len, ports)], mp32.at[:, pl.ds(r * ports, ports)], mp_sem.at[r]
        )

    for r in range(rows):
        mp_copy(r).start()

    def inv_copy(b):
        cols = pl.ds(pl.multiple_of(b * slice_len, LANES), slice_len)
        return pltpu.make_async_copy(inv.at[0, :, cols], m32.at[:, cols], inv_sem.at[b])

    for j in range(rows):
        inv_copy(lax.rem(me + j, rows)).start()

    for copy in small_copies:
        copy.wait()

    shifted = hist[0]
    shift = HISTORY - delay[...]
    bit = 1
    while bit <= HISTORY - STEPS:
        moved = pltpu.roll(shifted, HISTORY - bit, 0)
        shifted = jnp.where((shift // bit) % 2 == 1, moved, shifted)
        bit *= 2

    lane16a, row16a = iota((arrests, LANES), 1), iota((arrests, LANES), 0)
    lane16c, row16c = iota((cores, LANES), 1), iota((cores, LANES), 0)
    put_a = jnp.where(lane16a % elems == row16a, 1.0, 0.0).astype(BF16)
    put_c = jnp.where(lane16c % elems == row16c + arrests, 1.0, 0.0).astype(BF16)
    slot_a = jnp.broadcast_to(aslots[...].astype(F32), (8, arrests)).astype(BF16)
    slot_c = jnp.broadcast_to(cslots[...].astype(F32), (8, cores)).astype(BF16)
    slot_row = (dot(slot_a, put_a) + dot(slot_c, put_c))[0:1, :]
    hit = iota((ports, LANES), 0).astype(F32) == slot_row
    slot_tiled = jnp.where(hit, 1.0, 0.0)
    slot_own = jnp.where(iota((ports, LANES), 1) // elems == me % group, slot_tiled, 0.0)
    r8 = iota((8, ports), 0)
    params = jnp.where(
        r8 == TAGS,
        iota((8, ports), 1).astype(F32),
        jnp.where(
            r8 == TAGS + 1,
            again[...],
            jnp.where(r8 == TAGS + 2, cgain[...], jnp.where(r8 == TAGS + 3, prev[...], flux[...])),
        ),
    )
    p1 = params.astype(BF16).astype(F32)
    p2 = (params - p1).astype(BF16).astype(F32)
    parts = dot(jnp.concatenate([p1, p2, params - p1 - p2], axis=0).astype(BF16), slot_own.astype(BF16))
    par = (parts[:8] + parts[8:16]) + parts[16:24]
    k8 = iota((8, LANES), 0)
    tags = jnp.where(k8 == 0, dest[...], jnp.where(k8 == 1, port[...] // ports, port[...] % ports))
    unit[c, z, :STEPS, :] = shifted[:STEPS, :]
    unit[c, z, STEPS:, :] = jnp.where(k8 < TAGS, tags.astype(F32), par)

    def remote(ref_from, ref_to, send, recv, to_sub, to_row):
        return pltpu.make_async_remote_copy(
            src_ref=ref_from, dst_ref=ref_to, send_sem=send, recv_sem=recv,
            device_id=(to_sub, to_row), device_id_type=MESH,
        )

    def unit_copy(cc, zz, at, target):
        ref = unit.at[cc, zz]
        return remote(ref, ref, unit_send.at[at], unit_recv.at[cc, zz], s, target)

    def line_copy(k, b, way, target):
        ref = gath.at[k, b]
        return remote(ref, ref, line_send.at[k, b, way], line_recv.at[k, b], s, target)

    def sub_copy(j):
        return remote(
            unit.at[c], got_units.at[c, peers - j], sub_send.at[j - 1], sub_recv.at[peers - j],
            lax.rem(s + j, subs), me,
        )

    def both_copy(cc):
        return remote(got_units.at[cc], got_units.at[cc], both_send.at[0], both_recv.at[0], s, partner)

    def elem_copy(b, at, target):
        return remote(elem.at[b], elem.at[b], elem_send.at[at], elem_recv.at[b], s, target)

    def fst_copy(b, at, target):
        return remote(fst.at[b], fst.at[b], fst_send.at[at], fst_recv.at[b], s, target)

    for k in range(CHUNKS):
        src_copy(k).wait()
    pl.semaphore_wait(barrier, rows + subs - 2)

    for j in range(1, zn):
        unit_copy(c, z, zn + j - 1, lax.rem(z + j, zn) * 2 + c).start()
    unit_copy(c, z, z, partner).start()

    def own_ways(k, act):
        for hop in (2, 1):
            if hop < zn:
                @pl.when(z + hop < zn)
                def _():
                    act(line_copy(k, me, hop - 1, (z + hop) * 2 + c))

                @pl.when(z - hop >= 0)
                def _():
                    act(line_copy(k, me, hop + 1, (z - hop) * 2 + c))
        act(line_copy(k, me, 4, partner))

    for k in range(CHUNKS):
        own_ways(k, lambda copy: copy.start())

    for r in range(rows):
        mp_copy(r).wait()
    mp_hi, mp_lo = hi_lo(mp32[...])
    mp2[:ports, :] = mp_hi
    mp2[ports:, :] = mp_lo
    acc[...] = jnp.zeros_like(acc)
    hacc[...] = jnp.zeros_like(hacc)

    def split_block(j, carry):
        b = lax.rem(me + j, rows)
        inv_copy(b).wait()
        cols = pl.ds(pl.multiple_of(b * slice_len, LANES), slice_len)
        high, low = hi_lo(m32[:, cols])
        m2[:ports, cols] = high
        m2[ports:, cols] = low
        return carry

    def use_sources(b):
        for kind in range(CHUNKS):
            cols = pl.ds(pl.multiple_of(b * slice_len + kind * width, LANES), width)
            acc[...] += dot(stack_hi_lo(gath[kind, b]), m2[:, cols], NT)

    lax.fori_loop(0, rows, split_block, 0)
    use_sources(me)

    def pass_unit(j, carry):
        zz = lax.rem(z + j, zn)
        unit_copy(c, zz, 0, partner).wait_recv()
        unit_copy(c, zz, zz, partner).start()
        return carry

    lax.fori_loop(1, zn, pass_unit, 0)
    for j in range(1, subs):
        sub_copy(j).start()

    def turn(i):
        below = i % 2 == 0
        dist = i // 2 + 1
        zb = jnp.where(below, z - dist, z + dist)
        step = jnp.where(below, 1, -1)
        return zb, dist, step, jnp.logical_and(zb >= 0, zb < zn)

    def onward_ways(k, b, dist, step, act):
        for hop in (1, 2):
            zt = z + step * hop
            inside = jnp.logical_and(zt >= 0, zt < zn)

            @pl.when(jnp.logical_and(dist % 2 == 0, inside))
            def _():
                act(line_copy(k, b, hop - 1, zt * 2 + c))

    def forward(i):
        zb, dist, step, valid = turn(i)
        b = zb * 2 + c

        @pl.when(valid)
        def _():
            for k in range(CHUNKS):
                line_copy(k, b, 0, partner).wait_recv()
                onward_ways(k, b, dist, step, lambda copy: copy.start())
                line_copy(k, b, 4, partner).start()

    def consume(i):
        zb, dist, step, valid = turn(i)

        @pl.when(valid)
        def _():
            use_sources(zb * 2 + c)
            other = zb * 2 + (1 - c)
            for k in range(CHUNKS):
                line_copy(k, other, 4, partner).wait_recv()
            use_sources(other)

    for k in range(CHUNKS):
        line_copy(k, partner, 4, partner).wait_recv()
    use_sources(partner)

    for j in range(zn):
        zz = lax.rem(z + j, zn)
        unit_copy(1 - c, zz, 0, partner).wait_recv()
    all_par = jnp.concatenate(
        [
            sum(unit[(h * group + i) % 2, (h * group + i) // 2, STEPS:, :] for i in range(group))
            for h in range(halves)
        ],
        axis=1,
    )
    slots_all = all_par[TAGS : TAGS + 1, :]
    at_slot = iota((ports, total), 0).astype(F32) == slots_all
    owner_of = iota((ports, total), 1) // elems
    pick = None
    for r in range(rows):
        choose = jnp.where(jnp.logical_and(at_slot, owner_of == r), 1.0, 0.0).astype(BF16)
        term = dot(mp2[:, r * ports : (r + 1) * ports], choose)
        pick = term if pick is None else pick + term
    x2[...] = pick.astype(BF16)
    slot_cols = jnp.transpose(slot_tiled)[:elems].astype(BF16)
    elem[me] = dot(slot_cols, x2[:ports, :]) + dot(slot_cols, x2[ports:, :])
    for j in range(1, zn):
        elem_copy(me, zn + j - 1, lax.rem(z + j, zn) * 2 + c).start()
    elem_copy(me, z, partner).start()

    forward(0)
    forward(1)

    def ring(i, carry):
        forward(i + 2)
        consume(i)
        return carry

    lax.fori_loop(0, turns - 2, ring, 0)

    for j in range(1, subs):
        sub_copy(j).wait_recv()
    both_copy(c).start()

    def use_records(cc):
        blocks = [(x, zz) for zz in range(zn) for x in range(peers)]
        values = jnp.concatenate([got_units[cc, x, zz, :STEPS, :] for x, zz in blocks], axis=1)
        tag = jnp.concatenate([got_units[cc, x, zz, STEPS:, :] for x, zz in blocks], axis=1)
        owner = jnp.where(tag[0:1, :] == s.astype(F32), tag[1:2, :], -1.0)
        spot = tag[2:3, :]
        wide = values.shape[1]
        land = jnp.where(iota((ports, wide), 0).astype(F32) == spot, 1.0, 0.0).astype(BF16)
        high, low = hi_lo(values)
        wide_owner = jnp.broadcast_to(owner, (STEPS, wide))
        split = []
        for r in range(rows):
            mine = jnp.where(wide_owner == float(r), 1.0, 0.0).astype(BF16)
            split += [high * mine, low * mine]
        hacc[...] += dot(jnp.concatenate(split, axis=0), land, NT)

    use_records(c)

    def last(i, carry):
        consume(i)
        return carry

    lax.fori_loop(turns - 2, turns, last, 0)
    both_copy(1 - c).wait_recv()
    use_records(1 - c)

    landed = jnp.concatenate(
        [
            hacc[2 * r * STEPS : (2 * r + 1) * STEPS, :] + hacc[(2 * r + 1) * STEPS : (2 * r + 2) * STEPS, :]
            for r in range(rows)
        ],
        axis=1,
    )
    first = four_terms(acc[...] - dot(stack_hi_lo(landed), mp2[...], NT))
    mine = dot(stack_hi_lo(first), slot_own.astype(BF16))
    fst[me] = mine[:STEPS] + mine[STEPS:]
    for j in range(1, rows):
        fst_copy(me, j - 1, lax.rem(me + j, rows)).start()

    for j in range(1, zn):
        zb = lax.rem(z + j, zn)
        elem_copy(zb * 2 + c, 0, partner).wait_recv()
        elem_copy(zb * 2 + c, zb, partner).start()
    for j in range(zn):
        elem_copy(lax.rem(z + j, zn) * 2 + (1 - c), 0, partner).wait_recv()

    w = elem[...].reshape(total, total)
    self_row = jnp.sum(jnp.where(iota((total, total), 0) == iota((total, total), 1), w, 0.0), axis=0, keepdims=True)
    w_hi, w_lo = hi_lo(jnp.transpose(w))
    wc[:, :total] = w_hi
    wc[:, total:] = w_lo

    full = (8, total)
    is_arrest = iota(full, 1) % elems < arrests
    rowp = lambda i: jnp.broadcast_to(all_par[TAGS + i : TAGS + i + 1, :], full)
    arrest_gain = jnp.where(is_arrest, rowp(1), 0.0)
    core_gain = jnp.where(is_arrest, 0.0, rowp(2))
    elem_self = jnp.broadcast_to(self_row, full)
    volts0 = rowp(3)
    flux0 = rowp(4)
    put = jnp.where(jnp.logical_and(at_slot, owner_of == me), 1.0, 0.0).astype(BF16)
    here = dot(jnp.ones((8, total), BF16), put, NT)[0:1]

    for j in range(1, subs):
        sub_copy(j).wait_send()
    both_copy(c).wait_send()
    for k in range(CHUNKS):
        own_ways(k, lambda copy: copy.wait_send())

    def drain(i, carry):
        zb, dist, step, valid = turn(i)
        b = zb * 2 + c

        @pl.when(valid)
        def _():
            for k in range(CHUNKS):
                onward_ways(k, b, dist, step, lambda copy: copy.wait_send())
                line_copy(k, b, 4, partner).wait_send()

        return carry

    lax.fori_loop(0, turns, drain, 0)
    for at in range(2 * zn - 1):
        unit_copy(c, z, at, partner).wait_send()
        elem_copy(me, at, partner).wait_send()

    for j in range(1, rows):
        fst_copy(lax.rem(me + j, rows), j - 1, partner).wait_recv()
    fall[...] = jnp.concatenate(
        [sum(fst[h * group + i] for i in range(group)) for h in range(halves)], axis=1
    )

    def advance(t, carry):
        voltage, flux_now = carry
        first_now = jnp.broadcast_to(fall[pl.ds(t, 1), :], full)
        iterate = voltage
        for newton_pass in range(NEWTON):
            linked = flux_now + half_step * (iterate + voltage)
            ratio = iterate * (1.0 / knee_volts)
            rr = ratio * ratio
            ll = linked * linked
            current = arrest_gain * (iterate * (1.0 + rr)) + core_gain * (linked * (1.0 + cubic_term * ll))
            slope = arrest_gain * (1.0 + 3.0 * rr) + core_gain * (half_step + (half_step * 3.0 * cubic_term) * ll)
            recip = 1.0 / (1.0 + elem_self * slope)
            got = dot(stack_hi_lo(current), wc[...])
            coupled = got[:8, :total] + got[8:, :total] + got[:8, total:]
            iterate = iterate - (iterate - first_now + coupled) * recip
        vo[pl.ds(t, 1), :] = iterate[0:1]
        cu[pl.ds(t, 1), :] = current[0:1]
        return iterate, flux_now + half_step * (iterate + voltage)

    lax.fori_loop(0, STEPS, advance, (volts0, flux0), unroll=4)

    reach = four_terms(dot(stack_hi_lo(cu[...]), x2[...], NT))
    placed = dot(stack_hi_lo(vo[...]), put, NT)
    stacked = jnp.where(here > 0.5, placed[:STEPS] + placed[STEPS:], first - reach)
    out[:STEPS, :] = stacked
    summed = jnp.sum(stacked, axis=0, keepdims=True)
    last_flux = flux[...] + half_step * (prev[...] + 2.0 * summed - stacked[STEPS - 1 : STEPS])
    out[STEPS:, :] = jnp.broadcast_to(last_flux, (8, ports))
    for j in range(1, rows):
        fst_copy(me, j - 1, partner).wait_send()


def give(both, volts, last_flux):
    volts[0] = both[:STEPS, :]
    last_flux[...] = both[STEPS : STEPS + 1, :]


def on_device(subs, rows, *args):
    inverse, sources = args[0], args[1]
    ports = inverse.shape[1]
    order = inverse.shape[2]
    slice_len = sources.shape[2]
    arrests, cores = args[10].shape[1], args[11].shape[1]
    elems = arrests + cores
    total = rows * elems
    zn = rows // 2
    vmem = pl.BlockSpec(memory_space=pltpu.VMEM)
    hbm = pl.BlockSpec(memory_space=pl.ANY)
    dma = pltpu.SemaphoreType.DMA
    small = args[2:]
    both = pl.pallas_call(
        functools.partial(kernel, subs, rows, ports, slice_len, arrests, cores, len(small)),
        out_shape=jax.ShapeDtypeStruct((STEPS + 8, ports), F32),
        in_specs=[hbm] * len(args),
        out_specs=vmem,
        scratch_shapes=[pltpu.VMEM(a.shape, a.dtype) for a in small]
        + [
            pltpu.VMEM((ports, order), F32),
            pltpu.VMEM((2 * ports, order), BF16),
            pltpu.VMEM((ports, rows * ports), F32),
            pltpu.VMEM((2 * ports, rows * ports), BF16),
            pltpu.VMEM((CHUNKS, rows, STEPS, slice_len // CHUNKS), F32),
            pltpu.VMEM((2, zn, STEPS + 8, LANES), F32),
            pltpu.VMEM((2, subs - 1, zn, STEPS + 8, LANES), F32),
            pltpu.VMEM((rows, elems, total), F32),
            pltpu.VMEM((rows, STEPS, LANES), F32),
            pltpu.VMEM((2 * ports, total), BF16),
            pltpu.VMEM((total, 2 * total), BF16),
            pltpu.VMEM((STEPS, total), F32),
            pltpu.VMEM((STEPS, total), F32),
            pltpu.VMEM((STEPS, total), F32),
            pltpu.VMEM((2 * STEPS, 2 * ports), F32),
            pltpu.VMEM((2 * STEPS * rows, ports), F32),
            dma((len(small),)),
            dma((rows,)),
            dma((rows,)),
            dma((CHUNKS,)),
            dma((CHUNKS, rows, 5)),
            dma((CHUNKS, rows)),
            dma((2 * zn - 1,)),
            dma((2, zn)),
            dma((subs - 1,)),
            dma((subs - 1,)),
            dma((1,)),
            dma((1,)),
            dma((2 * zn - 1,)),
            dma((rows,)),
            dma((rows - 1,)),
            dma((rows,)),
        ],
        compiler_params=pltpu.CompilerParams(collective_id=0, has_side_effects=True),
        name="window",
    )(*args)
    return pl.pallas_call(
        give,
        out_shape=(
            jax.ShapeDtypeStruct((1, STEPS, ports), F32),
            jax.ShapeDtypeStruct((1, ports), F32),
        ),
        in_specs=[vmem],
        out_specs=(vmem, vmem),
        name="give",
    )(both)


def solution(mesh):
    subs, rows = mesh.shape["sub"], mesh.shape["row"]
    in_specs = (
        P("sub", "row", None),
        P("sub", None, "row"),
        P("sub", None, "row"),
    ) + (P("sub", "row"),) * 9
    out_specs = (P("sub", None, "row"), P("sub", "row"))
    return jax.shard_map(
        functools.partial(on_device, subs, rows),
        mesh=mesh, in_specs=in_specs, out_specs=out_specs, check_vma=False,
    )
```

```python
import functools

import jax
import jax.numpy as jnp
from jax import lax
from jax.experimental import pallas as pl
from jax.experimental.pallas import tpu as pltpu
from jax.sharding import PartitionSpec as P

STEPS = 16
HISTORY = 32
NEWTON = 2
LANES = 128
TAGS = 3

half_step = 0.25
knee_volts = 1.5
cubic_term = 0.25

F32 = jnp.float32
BF16 = jnp.bfloat16
MESH = pl.DeviceIdType.MESH
NN = (((1,), (0,)), ((), ()))
NT = (((1,), (1,)), ((), ()))
HIGHEST = lax.Precision.HIGHEST


def iota(shape, axis):
    return lax.broadcasted_iota(jnp.int32, shape, axis)


def hi_lo(x):
    high = x.astype(BF16)
    return high, (x - high.astype(F32)).astype(BF16)


def stack_hi_lo(x):
    return jnp.concatenate(hi_lo(x), axis=0)


def dot(a, b, dims=NN):
    return lax.dot_general(a, b, dims, preferred_element_type=F32)


def four_terms(r):
    n, m = r.shape[0] // 2, r.shape[1] // 2
    return (r[:n, :m] + r[n:, :m]) + (r[:n, m:] + r[n:, m:])


def kernel(
    subs, rows, ports, slice_len, arrests, cores, n_small,
    inv, src, *refs,
):
    small_hbm, refs = refs[:n_small], refs[n_small:]
    out, refs = refs[0], refs[1:]
    small, refs = refs[:n_small], refs[n_small:]
    (
        m32, m2, mp32, mp2, gath, unit, got_units, elem, fst, x2, wc, fall, vo, cu, acc, hacc,
        small_sem, inv_sem, mp_sem, src_sem, line_send, line_recv, unit_send, unit_recv,
        sub_send, sub_recv, both_send, both_recv, elem_send, elem_recv, fst_send, fst_recv,
    ) = refs
    hist, dest, port, delay, prev, flux, again, cgain, aslots, cslots = small
    s = lax.axis_index("sub")
    me = lax.axis_index("row")
    z, c = me // 2, me % 2
    zn = rows // 2
    partner = z * 2 + (1 - c)
    elems = arrests + cores
    group = LANES // elems
    total = rows * elems
    halves = total // LANES
    peers = subs - 1
    turns = 2 * (zn - 1)

    barrier = pltpu.get_barrier_semaphore()
    for j in range(1, rows):
        pl.semaphore_signal(barrier, inc=1, device_id=(s, lax.rem(me + j, rows)), device_id_type=MESH)
    for j in range(1, subs):
        pl.semaphore_signal(barrier, inc=1, device_id=(lax.rem(s + j, subs), me), device_id_type=MESH)

    small_copies = [
        pltpu.make_async_copy(small_hbm[i], small[i], small_sem.at[i]) for i in range(n_small)
    ]
    for copy in small_copies:
        copy.start()

    src_copy = pltpu.make_async_copy(src.at[0], gath.at[me], src_sem.at[0])
    src_copy.start()
    for copy in small_copies:
        copy.wait()

    def mp_copy(r):
        return pltpu.make_async_copy(
            inv.at[0, :, pl.ds(r * slice_len, ports)], mp32.at[:, pl.ds(r * ports, ports)], mp_sem.at[r]
        )

    for r in range(rows):
        mp_copy(r).start()

    def inv_copy(b):
        cols = pl.ds(pl.multiple_of(b * slice_len, LANES), slice_len)
        return pltpu.make_async_copy(inv.at[0, :, cols], m32.at[:, cols], inv_sem.at[b])

    for j in range(rows):
        inv_copy(lax.rem(me + j, rows)).start()

    shifted = hist[0]
    shift = HISTORY - delay[...]
    bit = 1
    while bit <= HISTORY - STEPS:
        moved = pltpu.roll(shifted, HISTORY - bit, 0)
        shifted = jnp.where((shift // bit) % 2 == 1, moved, shifted)
        bit *= 2

    lane16a, row16a = iota((arrests, LANES), 1), iota((arrests, LANES), 0)
    lane16c, row16c = iota((cores, LANES), 1), iota((cores, LANES), 0)
    put_a = jnp.where(lane16a % elems == row16a, 1.0, 0.0).astype(BF16)
    put_c = jnp.where(lane16c % elems == row16c + arrests, 1.0, 0.0).astype(BF16)
    slot_a = jnp.broadcast_to(aslots[...].astype(F32), (8, arrests)).astype(BF16)
    slot_c = jnp.broadcast_to(cslots[...].astype(F32), (8, cores)).astype(BF16)
    slot_row = (dot(slot_a, put_a) + dot(slot_c, put_c))[0:1, :]
    hit = iota((ports, LANES), 0).astype(F32) == slot_row
    slot_tiled = jnp.where(hit, 1.0, 0.0)
    slot_own = jnp.where(iota((ports, LANES), 1) // elems == me % group, slot_tiled, 0.0)
    r8 = iota((8, ports), 0)
    params = jnp.where(
        r8 == TAGS,
        iota((8, ports), 1).astype(F32),
        jnp.where(
            r8 == TAGS + 1,
            again[...],
            jnp.where(r8 == TAGS + 2, cgain[...], jnp.where(r8 == TAGS + 3, prev[...], flux[...])),
        ),
    )
    p1 = params.astype(BF16).astype(F32)
    p2 = (params - p1).astype(BF16).astype(F32)
    parts = dot(jnp.concatenate([p1, p2, params - p1 - p2], axis=0).astype(BF16), slot_own.astype(BF16))
    par = (parts[:8] + parts[8:16]) + parts[16:24]
    k8 = iota((8, LANES), 0)
    tags = jnp.where(k8 == 0, dest[...], jnp.where(k8 == 1, port[...] // ports, port[...] % ports))
    unit[c, z, :STEPS, :] = shifted[:STEPS, :]
    unit[c, z, STEPS:, :] = jnp.where(k8 < TAGS, tags.astype(F32), par)

    def remote(ref_from, ref_to, send, recv, to_sub, to_row):
        return pltpu.make_async_remote_copy(
            src_ref=ref_from, dst_ref=ref_to, send_sem=send, recv_sem=recv,
            device_id=(to_sub, to_row), device_id_type=MESH,
        )

    def unit_copy(cc, zz, at, target):
        ref = unit.at[cc, zz]
        return remote(ref, ref, unit_send.at[at], unit_recv.at[cc, zz], s, target)

    def line_copy(b, at, target):
        return remote(gath.at[b], gath.at[b], line_send.at[at], line_recv.at[b], s, target)

    def sub_copy(j):
        return remote(
            unit.at[c], got_units.at[c, peers - j], sub_send.at[j - 1], sub_recv.at[peers - j],
            lax.rem(s + j, subs), me,
        )

    def both_copy(cc):
        return remote(got_units.at[cc], got_units.at[cc], both_send.at[0], both_recv.at[0], s, partner)

    def elem_copy(b, at, target):
        return remote(elem.at[b], elem.at[b], elem_send.at[at], elem_recv.at[b], s, target)

    def fst_copy(b, at, target):
        return remote(fst.at[b], fst.at[b], fst_send.at[at], fst_recv.at[b], s, target)

    src_copy.wait()
    pl.semaphore_wait(barrier, rows + subs - 2)

    for j in range(1, zn):
        unit_copy(c, z, zn + j - 1, lax.rem(z + j, zn) * 2 + c).start()
    unit_copy(c, z, z, partner).start()

    def own_ways(act):
        for dist in range(zn - 1, 0, -1):
            @pl.when(z + dist < zn)
            def _():
                act(line_copy(me, zn + z + dist, (z + dist) * 2 + c))

            @pl.when(z - dist >= 0)
            def _():
                act(line_copy(me, zn + z - dist, (z - dist) * 2 + c))

    line_copy(me, z, partner).start()
    own_ways(lambda copy: copy.start())

    for r in range(rows):
        mp_copy(r).wait()
    mp_hi, mp_lo = hi_lo(mp32[...])
    mp2[:ports, :] = mp_hi
    mp2[ports:, :] = mp_lo
    acc[...] = jnp.zeros_like(acc)
    hacc[...] = jnp.zeros_like(hacc)

    def split_block(j, carry):
        b = lax.rem(me + j, rows)
        inv_copy(b).wait()
        cols = pl.ds(pl.multiple_of(b * slice_len, LANES), slice_len)
        high, low = hi_lo(m32[:, cols])
        m2[:ports, cols] = high
        m2[ports:, cols] = low
        return carry

    def use_sources(b):
        cols = pl.ds(pl.multiple_of(b * slice_len, LANES), slice_len)
        acc[...] += dot(stack_hi_lo(gath[b]), m2[:, cols], NT)

    lax.fori_loop(0, rows, split_block, 0)
    use_sources(me)

    def pass_unit(j, carry):
        zz = lax.rem(z + j, zn)
        unit_copy(c, zz, 0, partner).wait_recv()
        unit_copy(c, zz, zz, partner).start()
        return carry

    lax.fori_loop(1, zn, pass_unit, 0)
    for j in range(1, subs):
        sub_copy(j).start()

    def arrive(i, p):
        zb = jnp.where(i % 2 == 0, z - i // 2 - 1, z + i // 2 + 1)
        b = zb * 2 + p

        @pl.when(jnp.logical_and(zb >= 0, zb < zn))
        def _():
            line_copy(b, zb, partner).wait_recv()

            @pl.when(p == c)
            def _():
                line_copy(b, zb, partner).start()

            use_sources(b)

    line_copy(partner, z, partner).wait_recv()
    use_sources(partner)

    for j in range(zn):
        zz = lax.rem(z + j, zn)
        unit_copy(1 - c, zz, 0, partner).wait_recv()
    all_par = jnp.concatenate(
        [
            sum(unit[(h * group + i) % 2, (h * group + i) // 2, STEPS:, :] for i in range(group))
            for h in range(halves)
        ],
        axis=1,
    )
    slots_all = all_par[TAGS : TAGS + 1, :]
    at_slot = iota((ports, total), 0).astype(F32) == slots_all
    owner_of = iota((ports, total), 1) // elems
    pick = None
    for r in range(rows):
        choose = jnp.where(jnp.logical_and(at_slot, owner_of == r), 1.0, 0.0).astype(BF16)
        term = dot(mp2[:, r * ports : (r + 1) * ports], choose)
        pick = term if pick is None else pick + term
    x2[...] = pick.astype(BF16)
    slot_cols = jnp.transpose(slot_tiled)[:elems].astype(BF16)
    elem[me] = dot(slot_cols, x2[:ports, :]) + dot(slot_cols, x2[ports:, :])
    for j in range(1, zn):
        elem_copy(me, zn + j - 1, lax.rem(z + j, zn) * 2 + c).start()
    elem_copy(me, z, partner).start()

    def near_core(q, carry):
        arrive(turns - 1 - q, 1)
        return carry

    lax.fori_loop(0, turns, near_core, 0)

    for j in range(1, subs):
        sub_copy(j).wait_recv()
    both_copy(c).start()

    def use_records(cc):
        blocks = [(x, zz) for zz in range(zn) for x in range(peers)]
        values = jnp.concatenate([got_units[cc, x, zz, :STEPS, :] for x, zz in blocks], axis=1)
        tag = jnp.concatenate([got_units[cc, x, zz, STEPS:, :] for x, zz in blocks], axis=1)
        owner = jnp.where(tag[0:1, :] == s.astype(F32), tag[1:2, :], -1.0)
        spot = tag[2:3, :]
        wide = values.shape[1]
        land = jnp.where(iota((ports, wide), 0).astype(F32) == spot, 1.0, 0.0).astype(BF16)
        high, low = hi_lo(values)
        wide_owner = jnp.broadcast_to(owner, (STEPS, wide))
        split = []
        for r in range(rows):
            mine = jnp.where(wide_owner == float(r), 1.0, 0.0).astype(BF16)
            split += [high * mine, low * mine]
        hacc[...] += dot(jnp.concatenate(split, axis=0), land, NT)

    use_records(c)

    def far_core(q, carry):
        arrive(turns - 1 - q, 0)
        return carry

    lax.fori_loop(0, turns - 2, far_core, 0)
    both_copy(1 - c).wait_recv()
    use_records(1 - c)
    lax.fori_loop(turns - 2, turns, far_core, 0)

    landed = jnp.concatenate(
        [
            hacc[2 * r * STEPS : (2 * r + 1) * STEPS, :] + hacc[(2 * r + 1) * STEPS : (2 * r + 2) * STEPS, :]
            for r in range(rows)
        ],
        axis=1,
    )
    first = four_terms(acc[...] - dot(stack_hi_lo(landed), mp2[...], NT))
    mine = dot(stack_hi_lo(first), slot_own.astype(BF16))
    fst[me] = mine[:STEPS] + mine[STEPS:]
    for j in range(1, rows):
        fst_copy(me, j - 1, lax.rem(me + j, rows)).start()

    for j in range(1, zn):
        zb = lax.rem(z + j, zn)
        elem_copy(zb * 2 + c, 0, partner).wait_recv()
        elem_copy(zb * 2 + c, zb, partner).start()
    for j in range(zn):
        elem_copy(lax.rem(z + j, zn) * 2 + (1 - c), 0, partner).wait_recv()

    w = elem[...].reshape(total, total)
    self_row = jnp.sum(jnp.where(iota((total, total), 0) == iota((total, total), 1), w, 0.0), axis=0, keepdims=True)
    w_hi, w_lo = hi_lo(jnp.transpose(w))
    wc[:, :total] = w_hi
    wc[:, total:] = w_lo

    full = (8, total)
    is_arrest = iota(full, 1) % elems < arrests
    rowp = lambda i: jnp.broadcast_to(all_par[TAGS + i : TAGS + i + 1, :], full)
    arrest_gain = jnp.where(is_arrest, rowp(1), 0.0)
    core_gain = jnp.where(is_arrest, 0.0, rowp(2))
    elem_self = jnp.broadcast_to(self_row, full)
    volts0 = rowp(3)
    flux0 = rowp(4)
    put = jnp.where(jnp.logical_and(at_slot, owner_of == me), 1.0, 0.0).astype(BF16)
    here = dot(jnp.ones((8, total), BF16), put, NT)[0:1]

    for j in range(1, subs):
        sub_copy(j).wait_send()
    both_copy(c).wait_send()
    own_ways(lambda copy: copy.wait_send())
    for at in range(zn):
        line_copy(me, at, partner).wait_send()
    for at in range(2 * zn - 1):
        unit_copy(c, z, at, partner).wait_send()
        elem_copy(me, at, partner).wait_send()

    for j in range(1, rows):
        fst_copy(lax.rem(me + j, rows), j - 1, partner).wait_recv()
    fall[...] = jnp.concatenate(
        [sum(fst[h * group + i] for i in range(group)) for h in range(halves)], axis=1
    )

    def advance(t, carry):
        voltage, flux_now = carry
        first_now = jnp.broadcast_to(fall[pl.ds(t, 1), :], full)
        iterate = voltage
        for newton_pass in range(NEWTON):
            linked = flux_now + half_step * (iterate + voltage)
            ratio = iterate * (1.0 / knee_volts)
            rr = ratio * ratio
            ll = linked * linked
            current = arrest_gain * (iterate * (1.0 + rr)) + core_gain * (linked * (1.0 + cubic_term * ll))
            slope = arrest_gain * (1.0 + 3.0 * rr) + core_gain * (half_step + (half_step * 3.0 * cubic_term) * ll)
            recip = 1.0 / (1.0 + elem_self * slope)
            got = dot(stack_hi_lo(current), wc[...])
            coupled = got[:8, :total] + got[8:, :total] + got[:8, total:]
            iterate = iterate - (iterate - first_now + coupled) * recip
        vo[pl.ds(t, 1), :] = iterate[0:1]
        cu[pl.ds(t, 1), :] = current[0:1]
        return iterate, flux_now + half_step * (iterate + voltage)

    lax.fori_loop(0, STEPS, advance, (volts0, flux0), unroll=4)

    reach = four_terms(dot(stack_hi_lo(cu[...]), x2[...], NT))
    placed = dot(stack_hi_lo(vo[...]), put, NT)
    stacked = jnp.where(here > 0.5, placed[:STEPS] + placed[STEPS:], first - reach)
    out[:STEPS, :] = stacked
    summed = jnp.sum(stacked, axis=0, keepdims=True)
    last_flux = flux[...] + half_step * (prev[...] + 2.0 * summed - stacked[STEPS - 1 : STEPS])
    out[STEPS:, :] = jnp.broadcast_to(last_flux, (8, ports))
    for j in range(1, rows):
        fst_copy(me, j - 1, partner).wait_send()


def give(both, volts, last_flux):
    volts[0] = both[:STEPS, :]
    last_flux[...] = both[STEPS : STEPS + 1, :]


def on_device(subs, rows, *args):
    inverse, sources = args[0], args[1]
    ports = inverse.shape[1]
    order = inverse.shape[2]
    slice_len = sources.shape[2]
    arrests, cores = args[10].shape[1], args[11].shape[1]
    elems = arrests + cores
    total = rows * elems
    zn = rows // 2
    vmem = pl.BlockSpec(memory_space=pltpu.VMEM)
    hbm = pl.BlockSpec(memory_space=pl.ANY)
    dma = pltpu.SemaphoreType.DMA
    small = args[2:]
    both = pl.pallas_call(
        functools.partial(kernel, subs, rows, ports, slice_len, arrests, cores, len(small)),
        out_shape=pltpu.VMEM((STEPS + 8, ports), F32),
        in_specs=[hbm] * len(args),
        out_specs=vmem,
        scratch_shapes=[pltpu.VMEM(a.shape, a.dtype) for a in small]
        + [
            pltpu.VMEM((ports, order), F32),
            pltpu.VMEM((2 * ports, order), BF16),
            pltpu.VMEM((ports, rows * ports), F32),
            pltpu.VMEM((2 * ports, rows * ports), BF16),
            pltpu.VMEM((rows, STEPS, slice_len), F32),
            pltpu.VMEM((2, zn, STEPS + 8, LANES), F32),
            pltpu.VMEM((2, subs - 1, zn, STEPS + 8, LANES), F32),
            pltpu.VMEM((rows, elems, total), F32),
            pltpu.VMEM((rows, STEPS, LANES), F32),
            pltpu.VMEM((2 * ports, total), BF16),
            pltpu.VMEM((total, 2 * total), BF16),
            pltpu.VMEM((STEPS, total), F32),
            pltpu.VMEM((STEPS, total), F32),
            pltpu.VMEM((STEPS, total), F32),
            pltpu.VMEM((2 * STEPS, 2 * ports), F32),
            pltpu.VMEM((2 * STEPS * rows, ports), F32),
            dma((len(small),)),
            dma((rows,)),
            dma((rows,)),
            dma((1,)),
            dma((2 * zn,)),
            dma((rows,)),
            dma((2 * zn - 1,)),
            dma((2, zn)),
            dma((subs - 1,)),
            dma((subs - 1,)),
            dma((1,)),
            dma((1,)),
            dma((2 * zn - 1,)),
            dma((rows,)),
            dma((rows - 1,)),
            dma((rows,)),
        ],
        compiler_params=pltpu.CompilerParams(collective_id=0, has_side_effects=True),
        name="window",
    )(*args)
    return pl.pallas_call(
        give,
        out_shape=(
            jax.ShapeDtypeStruct((1, STEPS, ports), F32),
            jax.ShapeDtypeStruct((1, ports), F32),
        ),
        in_specs=[vmem],
        out_specs=(vmem, vmem),
        name="give",
    )(pltpu.with_memory_space_constraint(both, pltpu.VMEM))


def solution(mesh):
    subs, rows = mesh.shape["sub"], mesh.shape["row"]
    in_specs = (
        P("sub", "row", None),
        P("sub", None, "row"),
        P("sub", None, "row"),
    ) + (P("sub", "row"),) * 9
    out_specs = (P("sub", None, "row"), P("sub", "row"))
    return jax.shard_map(
        functools.partial(on_device, subs, rows),
        mesh=mesh, in_specs=in_specs, out_specs=out_specs, check_vma=False,
    )
```

```python
import functools

import jax
import jax.numpy as jnp
from jax import lax
from jax.experimental import pallas as pl
from jax.experimental.pallas import tpu as pltpu
from jax.sharding import PartitionSpec as P

STEPS = 16
HISTORY = 32
NEWTON = 2
LANES = 128
TAGS = 3

half_step = 0.25
knee_volts = 1.5
cubic_term = 0.25

F32 = jnp.float32
BF16 = jnp.bfloat16
MESH = pl.DeviceIdType.MESH
NN = (((1,), (0,)), ((), ()))
NT = (((1,), (1,)), ((), ()))
HIGHEST = lax.Precision.HIGHEST


def iota(shape, axis):
    return lax.broadcasted_iota(jnp.int32, shape, axis)


def hi_lo(x):
    high = x.astype(BF16)
    return high, (x - high.astype(F32)).astype(BF16)


def stack_hi_lo(x):
    return jnp.concatenate(hi_lo(x), axis=0)


def dot(a, b, dims=NN):
    return lax.dot_general(a, b, dims, preferred_element_type=F32)


def four_terms(r):
    n, m = r.shape[0] // 2, r.shape[1] // 2
    return (r[:n, :m] + r[n:, :m]) + (r[:n, m:] + r[n:, m:])


def kernel(
    subs, rows, ports, slice_len, arrests, cores, n_small,
    inv, src, *refs,
):
    small_hbm, refs = refs[:n_small], refs[n_small:]
    out, refs = refs[0], refs[1:]
    small, refs = refs[:n_small], refs[n_small:]
    (
        m32, m2, mp32, mp2, gath, unit, got_units, elem, fst, x2, wc, fall, vo, cu, acc, hacc,
        small_sem, inv_sem, mp_sem, src_sem, line_send, line_recv, unit_send, unit_recv,
        sub_send, sub_recv, both_send, both_recv, elem_send, elem_recv, fst_send, fst_recv,
    ) = refs
    hist, dest, port, delay, prev, flux, again, cgain, aslots, cslots = small
    s = lax.axis_index("sub")
    me = lax.axis_index("row")
    z, c = me // 2, me % 2
    zn = rows // 2
    partner = z * 2 + (1 - c)
    elems = arrests + cores
    group = LANES // elems
    total = rows * elems
    halves = total // LANES
    peers = subs - 1
    turns = 2 * (zn - 1)

    barrier = pltpu.get_barrier_semaphore()
    for j in range(1, rows):
        pl.semaphore_signal(barrier, inc=1, device_id=(s, lax.rem(me + j, rows)), device_id_type=MESH)
    for j in range(1, subs):
        pl.semaphore_signal(barrier, inc=1, device_id=(lax.rem(s + j, subs), me), device_id_type=MESH)

    small_copies = [
        pltpu.make_async_copy(small_hbm[i], small[i], small_sem.at[i]) for i in range(n_small)
    ]
    for copy in small_copies:
        copy.start()

    src_copy = pltpu.make_async_copy(src.at[0], gath.at[me], src_sem.at[0])
    src_copy.start()
    for copy in small_copies:
        copy.wait()

    def mp_copy(r):
        return pltpu.make_async_copy(
            inv.at[0, :, pl.ds(r * slice_len, ports)], mp32.at[:, pl.ds(r * ports, ports)], mp_sem.at[r]
        )

    for r in range(rows):
        mp_copy(r).start()

    def inv_copy(b):
        cols = pl.ds(pl.multiple_of(b * slice_len, LANES), slice_len)
        return pltpu.make_async_copy(inv.at[0, :, cols], m32.at[:, cols], inv_sem.at[b])

    for j in range(rows):
        inv_copy(lax.rem(me + j, rows)).start()

    shifted = hist[0]
    shift = HISTORY - delay[...]
    bit = 1
    while bit <= HISTORY - STEPS:
        moved = pltpu.roll(shifted, HISTORY - bit, 0)
        shifted = jnp.where((shift // bit) % 2 == 1, moved, shifted)
        bit *= 2

    lane16a, row16a = iota((arrests, LANES), 1), iota((arrests, LANES), 0)
    lane16c, row16c = iota((cores, LANES), 1), iota((cores, LANES), 0)
    put_a = jnp.where(lane16a % elems == row16a, 1.0, 0.0).astype(BF16)
    put_c = jnp.where(lane16c % elems == row16c + arrests, 1.0, 0.0).astype(BF16)
    slot_a = jnp.broadcast_to(aslots[...].astype(F32), (8, arrests)).astype(BF16)
    slot_c = jnp.broadcast_to(cslots[...].astype(F32), (8, cores)).astype(BF16)
    slot_row = (dot(slot_a, put_a) + dot(slot_c, put_c))[0:1, :]
    hit = iota((ports, LANES), 0).astype(F32) == slot_row
    slot_tiled = jnp.where(hit, 1.0, 0.0)
    slot_own = jnp.where(iota((ports, LANES), 1) // elems == me % group, slot_tiled, 0.0)
    r8 = iota((8, ports), 0)
    params = jnp.where(
        r8 == TAGS,
        iota((8, ports), 1).astype(F32),
        jnp.where(
            r8 == TAGS + 1,
            again[...],
            jnp.where(r8 == TAGS + 2, cgain[...], jnp.where(r8 == TAGS + 3, prev[...], flux[...])),
        ),
    )
    p1 = params.astype(BF16).astype(F32)
    p2 = (params - p1).astype(BF16).astype(F32)
    parts = dot(jnp.concatenate([p1, p2, params - p1 - p2], axis=0).astype(BF16), slot_own.astype(BF16))
    par = (parts[:8] + parts[8:16]) + parts[16:24]
    k8 = iota((8, LANES), 0)
    tags = jnp.where(k8 == 0, dest[...], jnp.where(k8 == 1, port[...] // ports, port[...] % ports))
    unit[c, z, :STEPS, :] = shifted[:STEPS, :]
    unit[c, z, STEPS:, :] = jnp.where(k8 < TAGS, tags.astype(F32), par)

    def remote(ref_from, ref_to, send, recv, to_sub, to_row):
        return pltpu.make_async_remote_copy(
            src_ref=ref_from, dst_ref=ref_to, send_sem=send, recv_sem=recv,
            device_id=(to_sub, to_row), device_id_type=MESH,
        )

    def unit_copy(cc, zz, at, target):
        ref = unit.at[cc, zz]
        return remote(ref, ref, unit_send.at[at], unit_recv.at[cc, zz], s, target)

    def line_copy(b, at, target):
        return remote(gath.at[b], gath.at[b], line_send.at[at], line_recv.at[b], s, target)

    def sub_copy(j):
        return remote(
            unit.at[c], got_units.at[c, peers - j], sub_send.at[j - 1], sub_recv.at[peers - j],
            lax.rem(s + j, subs), me,
        )

    def both_copy(cc):
        return remote(got_units.at[cc], got_units.at[cc], both_send.at[0], both_recv.at[0], s, partner)

    def elem_copy(b, at, target):
        return remote(elem.at[b], elem.at[b], elem_send.at[at], elem_recv.at[b], s, target)

    def fst_copy(b, at, target):
        return remote(fst.at[b], fst.at[b], fst_send.at[at], fst_recv.at[b], s, target)

    src_copy.wait()
    pl.semaphore_wait(barrier, rows + subs - 2)

    for j in range(1, zn):
        unit_copy(c, z, zn + j - 1, lax.rem(z + j, zn) * 2 + c).start()
    unit_copy(c, z, z, partner).start()

    def own_ways(act):
        for dist in range(zn - 1, 0, -1):
            @pl.when(z + dist < zn)
            def _():
                act(line_copy(me, zn + z + dist, (z + dist) * 2 + c))

            @pl.when(z - dist >= 0)
            def _():
                act(line_copy(me, zn + z - dist, (z - dist) * 2 + c))

    def send_sources(core):
        @pl.when(c == core)
        def _():
            own_ways(lambda copy: copy.start())
            line_copy(me, z, partner).start()

    send_sources(0)

    for r in range(rows):
        mp_copy(r).wait()
    mp_hi, mp_lo = hi_lo(mp32[...])
    mp2[:ports, :] = mp_hi
    mp2[ports:, :] = mp_lo
    send_sources(1)
    acc[...] = jnp.zeros_like(acc)
    hacc[...] = jnp.zeros_like(hacc)

    def split_block(j, carry):
        b = lax.rem(me + j, rows)
        inv_copy(b).wait()
        cols = pl.ds(pl.multiple_of(b * slice_len, LANES), slice_len)
        high, low = hi_lo(m32[:, cols])
        m2[:ports, cols] = high
        m2[ports:, cols] = low
        return carry

    def use_sources(b):
        cols = pl.ds(pl.multiple_of(b * slice_len, LANES), slice_len)
        acc[...] += dot(stack_hi_lo(gath[b]), m2[:, cols], NT)

    lax.fori_loop(0, rows, split_block, 0)
    use_sources(me)

    def pass_unit(j, carry):
        zz = lax.rem(z + j, zn)
        unit_copy(c, zz, 0, partner).wait_recv()
        unit_copy(c, zz, zz, partner).start()
        return carry

    lax.fori_loop(1, zn, pass_unit, 0)
    for j in range(1, subs):
        sub_copy(j).start()

    zfar = jnp.where(z < zn // 2, zn - 1, 0)

    def other_chips(act):
        def body(q, carry):
            i = turns - 1 - q
            zb = jnp.where(i % 2 == 0, z - i // 2 - 1, z + i // 2 + 1)

            @pl.when(jnp.logical_and(jnp.logical_and(zb >= 0, zb < zn), zb != zfar))
            def _():
                act(zb)

            return carry

        lax.fori_loop(0, turns, body, 0)

    def take(zb):
        line_copy(zb * 2 + c, zb, partner).wait_recv()
        line_copy(zb * 2 + c, zb, partner).start()

    def take_passed(zb):
        line_copy(zb * 2 + 1 - c, zb, partner).wait_recv()

    line_copy(partner, z, partner).wait_recv()
    use_sources(partner)

    def use_own(zb):
        use_sources(zb * 2 + c)

    def use_passed(zb):
        take_passed(zb)
        use_sources(zb * 2 + 1 - c)

    take(zfar)
    use_own(zfar)
    use_passed(zfar)

    for j in range(zn):
        zz = lax.rem(z + j, zn)
        unit_copy(1 - c, zz, 0, partner).wait_recv()
    all_par = jnp.concatenate(
        [
            sum(unit[(h * group + i) % 2, (h * group + i) // 2, STEPS:, :] for i in range(group))
            for h in range(halves)
        ],
        axis=1,
    )
    slots_all = all_par[TAGS : TAGS + 1, :]
    at_slot = iota((ports, total), 0).astype(F32) == slots_all
    owner_of = iota((ports, total), 1) // elems
    pick = None
    for r in range(rows):
        choose = jnp.where(jnp.logical_and(at_slot, owner_of == r), 1.0, 0.0).astype(BF16)
        term = dot(mp2[:, r * ports : (r + 1) * ports], choose)
        pick = term if pick is None else pick + term
    x2[...] = pick.astype(BF16)
    slot_cols = jnp.transpose(slot_tiled)[:elems].astype(BF16)
    elem[me] = dot(slot_cols, x2[:ports, :]) + dot(slot_cols, x2[ports:, :])
    for j in range(1, subs):
        sub_copy(j).wait_recv()
    both_copy(c).start()

    def use_records(cc):
        blocks = [(x, zz) for zz in range(zn) for x in range(peers)]
        values = jnp.concatenate([got_units[cc, x, zz, :STEPS, :] for x, zz in blocks], axis=1)
        tag = jnp.concatenate([got_units[cc, x, zz, STEPS:, :] for x, zz in blocks], axis=1)
        owner = jnp.where(tag[0:1, :] == s.astype(F32), tag[1:2, :], -1.0)
        spot = tag[2:3, :]
        wide = values.shape[1]
        land = jnp.where(iota((ports, wide), 0).astype(F32) == spot, 1.0, 0.0).astype(BF16)
        high, low = hi_lo(values)
        wide_owner = jnp.broadcast_to(owner, (STEPS, wide))
        split = []
        for r in range(rows):
            mine = jnp.where(wide_owner == float(r), 1.0, 0.0).astype(BF16)
            split += [high * mine, low * mine]
        hacc[...] += dot(jnp.concatenate(split, axis=0), land, NT)

    use_records(c)
    other_chips(take)
    for j in range(1, zn):
        elem_copy(me, zn + j - 1, lax.rem(z + j, zn) * 2 + c).start()
    elem_copy(me, z, partner).start()
    other_chips(use_own)
    both_copy(1 - c).wait_recv()
    use_records(1 - c)
    other_chips(use_passed)

    landed = jnp.concatenate(
        [
            hacc[2 * r * STEPS : (2 * r + 1) * STEPS, :] + hacc[(2 * r + 1) * STEPS : (2 * r + 2) * STEPS, :]
            for r in range(rows)
        ],
        axis=1,
    )
    first = four_terms(acc[...] - dot(stack_hi_lo(landed), mp2[...], NT))
    mine = dot(stack_hi_lo(first), slot_own.astype(BF16))
    fst[me] = mine[:STEPS] + mine[STEPS:]
    for j in range(1, rows):
        fst_copy(me, j - 1, lax.rem(me + j, rows)).start()

    for j in range(1, zn):
        zb = lax.rem(z + j, zn)
        elem_copy(zb * 2 + c, 0, partner).wait_recv()
        elem_copy(zb * 2 + c, zb, partner).start()
    for j in range(zn):
        elem_copy(lax.rem(z + j, zn) * 2 + (1 - c), 0, partner).wait_recv()

    w = elem[...].reshape(total, total)
    self_row = jnp.sum(jnp.where(iota((total, total), 0) == iota((total, total), 1), w, 0.0), axis=0, keepdims=True)
    w_hi, w_lo = hi_lo(jnp.transpose(w))
    wc[:, :total] = w_hi
    wc[:, total:] = w_lo

    full = (8, total)
    is_arrest = iota(full, 1) % elems < arrests
    rowp = lambda i: jnp.broadcast_to(all_par[TAGS + i : TAGS + i + 1, :], full)
    arrest_gain = jnp.where(is_arrest, rowp(1), 0.0)
    core_gain = jnp.where(is_arrest, 0.0, rowp(2))
    elem_self = jnp.broadcast_to(self_row, full)
    volts0 = rowp(3)
    flux0 = rowp(4)
    put = jnp.where(jnp.logical_and(at_slot, owner_of == me), 1.0, 0.0).astype(BF16)
    here = dot(jnp.ones((8, total), BF16), put, NT)[0:1]

    for j in range(1, subs):
        sub_copy(j).wait_send()
    both_copy(c).wait_send()
    own_ways(lambda copy: copy.wait_send())
    for at in range(zn):
        line_copy(me, at, partner).wait_send()
    for at in range(2 * zn - 1):
        unit_copy(c, z, at, partner).wait_send()
        elem_copy(me, at, partner).wait_send()

    for j in range(1, rows):
        fst_copy(lax.rem(me + j, rows), j - 1, partner).wait_recv()
    fall[...] = jnp.concatenate(
        [sum(fst[h * group + i] for i in range(group)) for h in range(halves)], axis=1
    )

    def advance(t, carry):
        voltage, flux_now = carry
        first_now = jnp.broadcast_to(fall[pl.ds(t, 1), :], full)
        iterate = voltage
        for newton_pass in range(NEWTON):
            linked = flux_now + half_step * (iterate + voltage)
            ratio = iterate * (1.0 / knee_volts)
            rr = ratio * ratio
            ll = linked * linked
            current = arrest_gain * (iterate * (1.0 + rr)) + core_gain * (linked * (1.0 + cubic_term * ll))
            slope = arrest_gain * (1.0 + 3.0 * rr) + core_gain * (half_step + (half_step * 3.0 * cubic_term) * ll)
            recip = 1.0 / (1.0 + elem_self * slope)
            got = dot(stack_hi_lo(current), wc[...])
            coupled = got[:8, :total] + got[8:, :total] + got[:8, total:]
            iterate = iterate - (iterate - first_now + coupled) * recip
        vo[pl.ds(t, 1), :] = iterate[0:1]
        cu[pl.ds(t, 1), :] = current[0:1]
        return iterate, flux_now + half_step * (iterate + voltage)

    lax.fori_loop(0, STEPS, advance, (volts0, flux0), unroll=4)

    reach = four_terms(dot(stack_hi_lo(cu[...]), x2[...], NT))
    placed = dot(stack_hi_lo(vo[...]), put, NT)
    stacked = jnp.where(here > 0.5, placed[:STEPS] + placed[STEPS:], first - reach)
    out[:STEPS, :] = stacked
    summed = jnp.sum(stacked, axis=0, keepdims=True)
    last_flux = flux[...] + half_step * (prev[...] + 2.0 * summed - stacked[STEPS - 1 : STEPS])
    out[STEPS:, :] = jnp.broadcast_to(last_flux, (8, ports))
    for j in range(1, rows):
        fst_copy(me, j - 1, partner).wait_send()


def give(both, volts, last_flux):
    volts[0] = both[:STEPS, :]
    last_flux[...] = both[STEPS : STEPS + 1, :]


def on_device(subs, rows, *args):
    inverse, sources = args[0], args[1]
    ports = inverse.shape[1]
    order = inverse.shape[2]
    slice_len = sources.shape[2]
    arrests, cores = args[10].shape[1], args[11].shape[1]
    elems = arrests + cores
    total = rows * elems
    zn = rows // 2
    vmem = pl.BlockSpec(memory_space=pltpu.VMEM)
    hbm = pl.BlockSpec(memory_space=pl.ANY)
    dma = pltpu.SemaphoreType.DMA
    small = args[2:]
    both = pl.pallas_call(
        functools.partial(kernel, subs, rows, ports, slice_len, arrests, cores, len(small)),
        out_shape=pltpu.VMEM((STEPS + 8, ports), F32),
        in_specs=[hbm] * len(args),
        out_specs=vmem,
        scratch_shapes=[pltpu.VMEM(a.shape, a.dtype) for a in small]
        + [
            pltpu.VMEM((ports, order), F32),
            pltpu.VMEM((2 * ports, order), BF16),
            pltpu.VMEM((ports, rows * ports), F32),
            pltpu.VMEM((2 * ports, rows * ports), BF16),
            pltpu.VMEM((rows, STEPS, slice_len), F32),
            pltpu.VMEM((2, zn, STEPS + 8, LANES), F32),
            pltpu.VMEM((2, subs - 1, zn, STEPS + 8, LANES), F32),
            pltpu.VMEM((rows, elems, total), F32),
            pltpu.VMEM((rows, STEPS, LANES), F32),
            pltpu.VMEM((2 * ports, total), BF16),
            pltpu.VMEM((total, 2 * total), BF16),
            pltpu.VMEM((STEPS, total), F32),
            pltpu.VMEM((STEPS, total), F32),
            pltpu.VMEM((STEPS, total), F32),
            pltpu.VMEM((2 * STEPS, 2 * ports), F32),
            pltpu.VMEM((2 * STEPS * rows, ports), F32),
            dma((len(small),)),
            dma((rows,)),
            dma((rows,)),
            dma((1,)),
            dma((2 * zn,)),
            dma((rows,)),
            dma((2 * zn - 1,)),
            dma((2, zn)),
            dma((subs - 1,)),
            dma((subs - 1,)),
            dma((1,)),
            dma((1,)),
            dma((2 * zn - 1,)),
            dma((rows,)),
            dma((rows - 1,)),
            dma((rows,)),
        ],
        compiler_params=pltpu.CompilerParams(collective_id=0, has_side_effects=True),
        name="window",
    )(*args)
    return pl.pallas_call(
        give,
        out_shape=(
            jax.ShapeDtypeStruct((1, STEPS, ports), F32),
            jax.ShapeDtypeStruct((1, ports), F32),
        ),
        in_specs=[vmem],
        out_specs=(vmem, vmem),
        name="give",
    )(pltpu.with_memory_space_constraint(both, pltpu.VMEM))


def solution(mesh):
    subs, rows = mesh.shape["sub"], mesh.shape["row"]
    in_specs = (
        P("sub", "row", None),
        P("sub", None, "row"),
        P("sub", None, "row"),
    ) + (P("sub", "row"),) * 9
    out_specs = (P("sub", None, "row"), P("sub", "row"))
    return jax.shard_map(
        functools.partial(on_device, subs, rows),
        mesh=mesh, in_specs=in_specs, out_specs=out_specs, check_vma=False,
    )
```

```python
import functools

import jax
import jax.numpy as jnp
from jax import lax
from jax.experimental import pallas as pl
from jax.experimental.pallas import tpu as pltpu
from jax.sharding import PartitionSpec as P

STEPS = 16
HISTORY = 32
NEWTON = 2
LANES = 128
TAGS = 3
HALVES = 2

half_step = 0.25
knee_volts = 1.5
cubic_term = 0.25

F32 = jnp.float32
BF16 = jnp.bfloat16
MESH = pl.DeviceIdType.MESH
NN = (((1,), (0,)), ((), ()))
NT = (((1,), (1,)), ((), ()))
HIGHEST = lax.Precision.HIGHEST


def iota(shape, axis):
    return lax.broadcasted_iota(jnp.int32, shape, axis)


def hi_lo(x):
    high = x.astype(BF16)
    return high, (x - high.astype(F32)).astype(BF16)


def stack_hi_lo(x):
    return jnp.concatenate(hi_lo(x), axis=0)


def dot(a, b, dims=NN):
    return lax.dot_general(a, b, dims, preferred_element_type=F32)


def four_terms(r):
    n, m = r.shape[0] // 2, r.shape[1] // 2
    return (r[:n, :m] + r[n:, :m]) + (r[:n, m:] + r[n:, m:])


def kernel(
    subs, rows, ports, slice_len, arrests, cores, n_small,
    inv, src, *refs,
):
    small_hbm, refs = refs[:n_small], refs[n_small:]
    (
        out, hist, tags_i, gains, slots, m32, m2, mp2, gath, unit, got_units, elem, fst,
        x2, wc, fall, vo, cu, acc, hacc,
        small_sem, inv_sem, line_sem, line_recv, unit_sem, sub_sem, both_sem, elem_sem, fst_sem,
    ) = refs
    s = lax.axis_index("sub")
    me = lax.axis_index("row")
    z, c = me // 2, me % 2
    zn = rows // 2
    partner = z * 2 + (1 - c)
    elems = arrests + cores
    group = LANES // elems
    total = rows * elems
    halves = total // LANES
    peers = subs - 1
    turns = 2 * (zn - 1)

    barrier = pltpu.get_barrier_semaphore()
    for j in range(1, rows):
        pl.semaphore_signal(barrier, inc=1, device_id=(s, lax.rem(me + j, rows)), device_id_type=MESH)
    for j in range(1, subs):
        pl.semaphore_signal(barrier, inc=1, device_id=(lax.rem(s + j, subs), me), device_id_type=MESH)

    ints, floats = small_hbm[1:4], small_hbm[4:8]
    pltpu.make_async_copy(small_hbm[0], hist, small_sem.at[0]).start()
    for i, ref in enumerate(ints):
        pltpu.make_async_copy(ref, tags_i.at[pl.ds(i, 1)], small_sem.at[1]).start()
    for i, ref in enumerate(floats):
        pltpu.make_async_copy(ref, gains.at[pl.ds(i, 1)], small_sem.at[2]).start()
    for i, ref in enumerate(small_hbm[8:]):
        pltpu.make_async_copy(ref, slots.at[i], small_sem.at[3]).start()
    src_copy = pltpu.make_async_copy(src.at[0], gath.at[me], small_sem.at[4])
    src_copy.start()

    def wait_all(ref, sem):
        pltpu.make_async_copy(ref, ref, sem).wait()

    wait_all(hist, small_sem.at[0])
    wait_all(tags_i.at[pl.ds(0, len(ints))], small_sem.at[1])
    wait_all(gains.at[pl.ds(0, len(floats))], small_sem.at[2])
    wait_all(slots, small_sem.at[3])
    dest, port, delay = (tags_i[i : i + 1, :] for i in range(len(ints)))
    prev, flux, again, cgain = (gains[i : i + 1, :] for i in range(len(floats)))

    span = m32.shape[1] // HALVES

    def inv_copy(h):
        cols = pl.ds(h * span, span)
        return pltpu.make_async_copy(inv.at[0, :, cols], m32.at[:, cols], inv_sem.at[h])

    for h in range(HALVES):
        inv_copy(h).start()

    shifted = hist[0]
    shift = HISTORY - delay
    bit = 1
    while bit <= HISTORY - STEPS:
        moved = pltpu.roll(shifted, HISTORY - bit, 0)
        shifted = jnp.where((shift // bit) % 2 == 1, moved, shifted)
        bit *= 2

    lane16a, row16a = iota((arrests, LANES), 1), iota((arrests, LANES), 0)
    lane16c, row16c = iota((cores, LANES), 1), iota((cores, LANES), 0)
    put_a = jnp.where(lane16a % elems == row16a, 1.0, 0.0).astype(BF16)
    put_c = jnp.where(lane16c % elems == row16c + arrests, 1.0, 0.0).astype(BF16)
    slot_a = jnp.broadcast_to(slots[0].astype(F32), (8, arrests)).astype(BF16)
    slot_c = jnp.broadcast_to(slots[1].astype(F32), (8, cores)).astype(BF16)
    slot_row = (dot(slot_a, put_a) + dot(slot_c, put_c))[0:1, :]
    hit = iota((ports, LANES), 0).astype(F32) == slot_row
    slot_tiled = jnp.where(hit, 1.0, 0.0)
    slot_own = jnp.where(iota((ports, LANES), 1) // elems == me % group, slot_tiled, 0.0)
    r8 = iota((8, ports), 0)
    params = jnp.where(
        r8 == TAGS,
        iota((8, ports), 1).astype(F32),
        jnp.where(
            r8 == TAGS + 1,
            again,
            jnp.where(r8 == TAGS + 2, cgain, jnp.where(r8 == TAGS + 3, prev, flux)),
        ),
    )
    p1 = params.astype(BF16).astype(F32)
    p2 = (params - p1).astype(BF16).astype(F32)
    parts = dot(jnp.concatenate([p1, p2, params - p1 - p2], axis=0).astype(BF16), slot_own.astype(BF16))
    par = (parts[:8] + parts[8:16]) + parts[16:24]
    k8 = iota((8, LANES), 0)
    tags = jnp.where(k8 == 0, dest, jnp.where(k8 == 1, port // ports, port % ports))
    mine_at = c * zn + z
    unit[mine_at, :STEPS, :] = shifted[:STEPS, :]
    unit[mine_at, STEPS:, :] = jnp.where(k8 < TAGS, tags.astype(F32), par)

    def remote(ref_from, ref_to, send, recv, to_sub, to_row):
        return pltpu.make_async_remote_copy(
            src_ref=ref_from, dst_ref=ref_to, send_sem=send, recv_sem=recv,
            device_id=(to_sub, to_row), device_id_type=MESH,
        )

    def unit_copy(zz, kind, target):
        ref = unit.at[c * zn + zz]
        return remote(ref, ref, unit_sem.at[0], unit_sem.at[1 + kind], s, target)

    def line_copy(b, target):
        return remote(gath.at[b], gath.at[b], line_sem.at[0], line_recv.at[b], s, target)

    def pass_copy(b):
        return remote(gath.at[b], gath.at[b], line_sem.at[1], line_recv.at[b], s, partner)

    def sub_copy(j):
        return remote(
            unit.at[pl.ds(c * zn, zn)], got_units.at[c, peers - j], sub_sem.at[0], sub_sem.at[1],
            lax.rem(s + j, subs), me,
        )

    def both_copy(cc):
        return remote(got_units.at[cc], got_units.at[cc], both_sem.at[0], both_sem.at[1], s, partner)

    def elem_copy(b, kind, target):
        return remote(elem.at[b], elem.at[b], elem_sem.at[0], elem_sem.at[1 + kind], s, target)

    def fst_copy(target):
        return remote(fst.at[me], fst.at[me], fst_sem.at[0], fst_sem.at[1], s, target)

    def sent(ref, sem):
        remote(ref, ref, sem, sem, s, partner).wait_send()

    def arrived(ref, sem):
        remote(ref, ref, sem, sem, s, partner).wait_recv()

    src_copy.wait()
    pl.semaphore_wait(barrier, rows + subs - 2)

    for j in range(1, zn):
        unit_copy(z, 0, lax.rem(z + j, zn) * 2 + c).start()
    unit_copy(z, 1, partner).start()

    for dist in [1] + list(range(zn - 1, 1, -1)):
        up, down = z + dist, z - dist

        @pl.when(jnp.logical_and(up < zn, jnp.logical_or(dist != 2, up != zn - 1)))
        def _():
            line_copy(me, up * 2 + c).start()

        @pl.when(jnp.logical_and(down >= 0, jnp.logical_or(dist != 2, down != 0)))
        def _():
            line_copy(me, down * 2 + c).start()

    pass_copy(me).start()
    lower, upper = z == 1, z == zn - 2
    relays = jnp.logical_or(lower, upper)
    skips = jnp.logical_or(z == 2, z == zn - 3)
    znear = jnp.where(z < zn // 2, z + 1, z - 1)

    acc[...] = jnp.zeros_like(acc)
    hacc[...] = jnp.zeros_like(hacc)

    def split_block(b, carry):
        cols = pl.ds(pl.multiple_of(b * slice_len, LANES), slice_len)
        high, low = hi_lo(m32[:, cols])
        m2[:ports, cols] = high
        m2[ports:, cols] = low
        at_ports = pl.ds(pl.multiple_of(b * ports, LANES), ports)
        mp2[:ports, at_ports] = high[:, :ports]
        mp2[ports:, at_ports] = low[:, :ports]
        return carry

    def use_sources(b):
        cols = pl.ds(pl.multiple_of(b * slice_len, LANES), slice_len)
        acc[...] += dot(stack_hi_lo(gath[b]), m2[:, cols], NT)

    for h in range(HALVES):
        inv_copy(h).wait()
        lax.fori_loop(h * rows // HALVES, (h + 1) * rows // HALVES, split_block, 0)
    use_sources(me)

    arrived(unit.at[pl.ds(0, zn - 1)], unit_sem.at[1])
    for j in range(1, zn):
        unit_copy(lax.rem(z + j, zn), 1, partner).start()
    for j in range(1, subs):
        sub_copy(j).start()

    def other_chips(lo, hi, act):
        def body(q, carry):
            i = jnp.where(jnp.logical_or(z == 0, z == zn - 1), turns - 1 - q, q)
            zb = jnp.where(i % 2 == 0, z - i // 2 - 1, z + i // 2 + 1)

            @pl.when(jnp.logical_and(jnp.logical_and(zb >= 0, zb < zn), zb != znear))
            def _():
                act(zb)

            return carry

        lax.fori_loop(lo, hi, body, 0)

    def take(zb):
        line_copy(zb * 2 + c, partner).wait_recv()
        pass_copy(zb * 2 + c).start()

    def use_own(zb):
        use_sources(zb * 2 + c)

    def use_passed(zb):
        pass_copy(zb * 2 + 1 - c).wait_recv()
        use_sources(zb * 2 + 1 - c)

    use_passed(z)
    line_copy(znear * 2 + c, partner).wait_recv()

    @pl.when(relays)
    def _():
        line_copy(znear * 2 + c, jnp.where(lower, z - 1, z + 1) * 2 + c).start()

    pass_copy(znear * 2 + c).start()
    use_own(znear)
    use_passed(znear)

    arrived(unit.at[pl.ds(0, zn)], unit_sem.at[2])
    all_par = jnp.concatenate(
        [
            sum(unit[(h * group + i) % 2 * zn + (h * group + i) // 2, STEPS:, :] for i in range(group))
            for h in range(halves)
        ],
        axis=1,
    )
    slots_all = all_par[TAGS : TAGS + 1, :]
    at_slot = iota((ports, total), 0).astype(F32) == slots_all
    owner_of = iota((ports, total), 1) // elems
    pick = None
    for r in range(rows):
        choose = jnp.where(jnp.logical_and(at_slot, owner_of == r), 1.0, 0.0).astype(BF16)
        term = dot(mp2[:, r * ports : (r + 1) * ports], choose)
        pick = term if pick is None else pick + term
    x2[...] = pick.astype(BF16)
    slot_cols = jnp.transpose(slot_tiled)[:elems].astype(BF16)
    elem[me] = dot(slot_cols, x2[:ports, :]) + dot(slot_cols, x2[ports:, :])
    for j in range(1, zn):
        elem_copy(me, 0, lax.rem(z + j, zn) * 2 + c).start()
    elem_copy(me, 1, partner).start()

    arrived(got_units.at[c], sub_sem.at[1])
    both_copy(c).start()

    def use_records(cc):
        blocks = [(x, zz) for zz in range(zn) for x in range(peers)]
        values = jnp.concatenate([got_units[cc, x, zz, :STEPS, :] for x, zz in blocks], axis=1)
        tag = jnp.concatenate([got_units[cc, x, zz, STEPS:, :] for x, zz in blocks], axis=1)
        owner = jnp.where(tag[0:1, :] == s.astype(F32), tag[1:2, :], -1.0)
        spot = tag[2:3, :]
        wide = values.shape[1]
        land = jnp.where(iota((ports, wide), 0).astype(F32) == spot, 1.0, 0.0).astype(BF16)
        high, low = hi_lo(values)
        wide_owner = jnp.broadcast_to(owner, (STEPS, wide))
        split = []
        for r in range(rows):
            mine = jnp.where(wide_owner == float(r), 1.0, 0.0).astype(BF16)
            split += [high * mine, low * mine]
        hacc[...] += dot(jnp.concatenate(split, axis=0), land, NT)

    use_records(c)

    def take_use(zb):
        take(zb)
        use_own(zb)

    other_chips(0, 2, take_use)
    both_copy(1 - c).wait_recv()
    use_records(1 - c)
    other_chips(2, turns, take_use)
    other_chips(0, turns, use_passed)

    landed = jnp.concatenate(
        [
            hacc[2 * r * STEPS : (2 * r + 1) * STEPS, :] + hacc[(2 * r + 1) * STEPS : (2 * r + 2) * STEPS, :]
            for r in range(rows)
        ],
        axis=1,
    )
    first = four_terms(acc[...] - dot(stack_hi_lo(landed), mp2[...], NT))
    mine = dot(stack_hi_lo(first), slot_own.astype(BF16))
    fst[me] = mine[:STEPS] + mine[STEPS:]
    for j in range(1, rows):
        fst_copy(lax.rem(me + j, rows)).start()

    arrived(elem.at[pl.ds(0, zn - 1)], elem_sem.at[1])
    for j in range(1, zn):
        elem_copy(lax.rem(z + j, zn) * 2 + c, 1, partner).start()
    arrived(elem.at[pl.ds(0, zn)], elem_sem.at[2])

    w = elem[...].reshape(total, total)
    self_row = jnp.sum(jnp.where(iota((total, total), 0) == iota((total, total), 1), w, 0.0), axis=0, keepdims=True)
    w_hi, w_lo = hi_lo(jnp.transpose(w))
    wc[:, :total] = w_hi
    wc[:, total:] = w_lo

    full = (8, total)
    is_arrest = iota(full, 1) % elems < arrests
    rowp = lambda i: jnp.broadcast_to(all_par[TAGS + i : TAGS + i + 1, :], full)
    arrest_gain = jnp.where(is_arrest, rowp(1), 0.0)
    core_gain = jnp.where(is_arrest, 0.0, rowp(2))
    elem_self = jnp.broadcast_to(self_row, full)
    volts0 = rowp(3)
    flux0 = rowp(4)
    put = jnp.where(jnp.logical_and(at_slot, owner_of == me), 1.0, 0.0).astype(BF16)
    here = dot(jnp.ones((8, total), BF16), put, NT)[0:1]

    sent(got_units.at[c], sub_sem.at[0])
    sent(got_units.at[c], both_sem.at[0])
    sent(gath.at[pl.ds(0, zn)], line_sem.at[1])
    line_sends = zn - 1 + relays.astype(jnp.int32) - skips.astype(jnp.int32)
    for n in range(zn - 2, zn + 1):
        @pl.when(line_sends == n)
        def _():
            sent(gath.at[pl.ds(0, n)], line_sem.at[0])

    sent(unit.at[pl.ds(0, 2 * zn - 1)], unit_sem.at[0])
    sent(elem.at[pl.ds(0, 2 * zn - 1)], elem_sem.at[0])
    arrived(fst.at[pl.ds(0, rows - 1)], fst_sem.at[1])
    fall[...] = jnp.concatenate(
        [sum(fst[h * group + i] for i in range(group)) for h in range(halves)], axis=1
    )

    def advance(t, carry):
        voltage, flux_now = carry
        first_now = jnp.broadcast_to(fall[pl.ds(t, 1), :], full)
        iterate = voltage
        for newton_pass in range(NEWTON):
            linked = flux_now + half_step * (iterate + voltage)
            ratio = iterate * (1.0 / knee_volts)
            rr = ratio * ratio
            ll = linked * linked
            current = arrest_gain * (iterate * (1.0 + rr)) + core_gain * (linked * (1.0 + cubic_term * ll))
            slope = arrest_gain * (1.0 + 3.0 * rr) + core_gain * (half_step + (half_step * 3.0 * cubic_term) * ll)
            recip = 1.0 / (1.0 + elem_self * slope)
            got = dot(stack_hi_lo(current), wc[...])
            coupled = got[:8, :total] + got[8:, :total] + got[:8, total:]
            iterate = iterate - (iterate - first_now + coupled) * recip
        vo[pl.ds(t, 1), :] = iterate[0:1]
        cu[pl.ds(t, 1), :] = current[0:1]
        return iterate, flux_now + half_step * (iterate + voltage)

    lax.fori_loop(0, STEPS, advance, (volts0, flux0), unroll=4)

    reach = four_terms(dot(stack_hi_lo(cu[...]), x2[...], NT))
    placed = dot(stack_hi_lo(vo[...]), put, NT)
    stacked = jnp.where(here > 0.5, placed[:STEPS] + placed[STEPS:], first - reach)
    out[:STEPS, :] = stacked
    summed = jnp.sum(stacked, axis=0, keepdims=True)
    last_flux = flux + half_step * (prev + 2.0 * summed - stacked[STEPS - 1 : STEPS])
    out[STEPS:, :] = jnp.broadcast_to(last_flux, (8, ports))
    sent(fst.at[pl.ds(0, rows - 1)], fst_sem.at[0])


def give(both, volts, last_flux):
    volts[0] = both[:STEPS, :]
    last_flux[...] = both[STEPS : STEPS + 1, :]


def on_device(subs, rows, *args):
    inverse, sources = args[0], args[1]
    ports = inverse.shape[1]
    order = inverse.shape[2]
    slice_len = sources.shape[2]
    arrests, cores = args[10].shape[1], args[11].shape[1]
    elems = arrests + cores
    total = rows * elems
    zn = rows // 2
    vmem = pl.BlockSpec(memory_space=pltpu.VMEM)
    hbm = pl.BlockSpec(memory_space=pl.ANY)
    dma = pltpu.SemaphoreType.DMA
    small = args[2:]
    both = pl.pallas_call(
        functools.partial(kernel, subs, rows, ports, slice_len, arrests, cores, len(small)),
        out_shape=pltpu.VMEM((STEPS + 8, ports), F32),
        in_specs=[hbm] * len(args),
        out_specs=vmem,
        scratch_shapes=[
            pltpu.VMEM(small[0].shape, F32),
            pltpu.VMEM((8, LANES), jnp.int32),
            pltpu.VMEM((8, LANES), F32),
            pltpu.VMEM((2, 1, arrests), jnp.int32),
            pltpu.VMEM((ports, order), F32),
            pltpu.VMEM((2 * ports, order), BF16),
            pltpu.VMEM((2 * ports, rows * ports), BF16),
            pltpu.VMEM((rows, STEPS, slice_len), F32),
            pltpu.VMEM((2 * zn, STEPS + 8, LANES), F32),
            pltpu.VMEM((2, subs - 1, zn, STEPS + 8, LANES), F32),
            pltpu.VMEM((rows, elems, total), F32),
            pltpu.VMEM((rows, STEPS, LANES), F32),
            pltpu.VMEM((2 * ports, total), BF16),
            pltpu.VMEM((total, 2 * total), BF16),
            pltpu.VMEM((STEPS, total), F32),
            pltpu.VMEM((STEPS, total), F32),
            pltpu.VMEM((STEPS, total), F32),
            pltpu.VMEM((2 * STEPS, 2 * ports), F32),
            pltpu.VMEM((2 * STEPS * rows, ports), F32),
            dma((5,)),
            dma((HALVES,)),
            dma((2,)),
            dma((rows,)),
            dma((3,)),
            dma((2,)),
            dma((2,)),
            dma((3,)),
            dma((2,)),
        ],
        compiler_params=pltpu.CompilerParams(collective_id=0, has_side_effects=True),
        name="window",
    )(*args)
    return pl.pallas_call(
        give,
        out_shape=(
            jax.ShapeDtypeStruct((1, STEPS, ports), F32),
            jax.ShapeDtypeStruct((1, ports), F32),
        ),
        in_specs=[vmem],
        out_specs=(vmem, vmem),
        name="give",
    )(pltpu.with_memory_space_constraint(both, pltpu.VMEM))


def solution(mesh):
    subs, rows = mesh.shape["sub"], mesh.shape["row"]
    in_specs = (
        P("sub", "row", None),
        P("sub", None, "row"),
        P("sub", None, "row"),
    ) + (P("sub", "row"),) * 9
    out_specs = (P("sub", None, "row"), P("sub", "row"))
    return jax.shard_map(
        functools.partial(on_device, subs, rows),
        mesh=mesh, in_specs=in_specs, out_specs=out_specs, check_vma=False,
    )
```

```python
import functools

import jax
import jax.numpy as jnp
from jax import lax
from jax.experimental import pallas as pl
from jax.experimental.pallas import tpu as pltpu
from jax.sharding import PartitionSpec as P

STEPS = 16
HISTORY = 32
NEWTON = 2
LANES = 128
TAGS = 3
HALVES = 2

half_step = 0.25
knee_volts = 1.5
cubic_term = 0.25

F32 = jnp.float32
BF16 = jnp.bfloat16
MESH = pl.DeviceIdType.MESH
NN = (((1,), (0,)), ((), ()))
NT = (((1,), (1,)), ((), ()))
HIGHEST = lax.Precision.HIGHEST


def iota(shape, axis):
    return lax.broadcasted_iota(jnp.int32, shape, axis)


def hi_lo(x):
    high = x.astype(BF16)
    return high, (x - high.astype(F32)).astype(BF16)


def stack_hi_lo(x):
    return jnp.concatenate(hi_lo(x), axis=0)


def dot(a, b, dims=NN):
    return lax.dot_general(a, b, dims, preferred_element_type=F32)


def four_terms(r):
    n, m = r.shape[0] // 2, r.shape[1] // 2
    return (r[:n, :m] + r[n:, :m]) + (r[:n, m:] + r[n:, m:])


def kernel(
    subs, rows, ports, slice_len, arrests, cores, n_small,
    inv, src, *refs,
):
    small_hbm, refs = refs[:n_small], refs[n_small:]
    (
        out, hist, tags_i, gains, slots, m32, m2, mp2, gath, unit, got_units, elem, fst,
        x2, wc, fall, vo, cu, acc, hacc,
        small_sem, inv_sem, line_sem, line_recv, unit_sem, sub_sem, sub_in, both_sem, elem_sem, fst_sem,
    ) = refs
    s = lax.axis_index("sub")
    me = lax.axis_index("row")
    z, c = me // 2, me % 2
    zn = rows // 2
    partner = z * 2 + (1 - c)
    elems = arrests + cores
    group = LANES // elems
    total = rows * elems
    halves = total // LANES
    peers = subs - 1
    turns = 2 * (zn - 1)

    barrier = pltpu.get_barrier_semaphore()
    for j in range(1, rows):
        pl.semaphore_signal(barrier, inc=1, device_id=(s, lax.rem(me + j, rows)), device_id_type=MESH)
    bits = [1 << k for k in range((subs - 1).bit_length())]
    for bit in bits:
        pl.semaphore_signal(barrier, inc=1, device_id=(s ^ bit, me), device_id_type=MESH)

    ints, floats = small_hbm[1:4], small_hbm[4:8]
    pltpu.make_async_copy(small_hbm[0], hist, small_sem.at[0]).start()
    for i, ref in enumerate(ints):
        pltpu.make_async_copy(ref, tags_i.at[pl.ds(i, 1)], small_sem.at[1]).start()
    for i, ref in enumerate(floats):
        pltpu.make_async_copy(ref, gains.at[pl.ds(i, 1)], small_sem.at[2]).start()
    for i, ref in enumerate(small_hbm[8:]):
        pltpu.make_async_copy(ref, slots.at[i], small_sem.at[3]).start()
    src_copy = pltpu.make_async_copy(src.at[0], gath.at[me], small_sem.at[4])
    src_copy.start()

    def wait_all(ref, sem):
        pltpu.make_async_copy(ref, ref, sem).wait()

    wait_all(hist, small_sem.at[0])
    wait_all(tags_i.at[pl.ds(0, len(ints))], small_sem.at[1])
    wait_all(gains.at[pl.ds(0, len(floats))], small_sem.at[2])
    wait_all(slots, small_sem.at[3])
    dest, port, delay = (tags_i[i : i + 1, :] for i in range(len(ints)))
    prev, flux, again, cgain = (gains[i : i + 1, :] for i in range(len(floats)))

    span = m32.shape[1] // HALVES

    def inv_copy(h):
        cols = pl.ds(h * span, span)
        return pltpu.make_async_copy(inv.at[0, :, cols], m32.at[:, cols], inv_sem.at[h])

    for h in range(HALVES):
        inv_copy(h).start()

    shifted = hist[0]
    shift = HISTORY - delay
    bit = 1
    while bit <= HISTORY - STEPS:
        moved = pltpu.roll(shifted, HISTORY - bit, 0)
        shifted = jnp.where((shift // bit) % 2 == 1, moved, shifted)
        bit *= 2

    lane16a, row16a = iota((arrests, LANES), 1), iota((arrests, LANES), 0)
    lane16c, row16c = iota((cores, LANES), 1), iota((cores, LANES), 0)
    put_a = jnp.where(lane16a % elems == row16a, 1.0, 0.0).astype(BF16)
    put_c = jnp.where(lane16c % elems == row16c + arrests, 1.0, 0.0).astype(BF16)
    slot_a = jnp.broadcast_to(slots[0].astype(F32), (8, arrests)).astype(BF16)
    slot_c = jnp.broadcast_to(slots[1].astype(F32), (8, cores)).astype(BF16)
    slot_row = (dot(slot_a, put_a) + dot(slot_c, put_c))[0:1, :]
    hit = iota((ports, LANES), 0).astype(F32) == slot_row
    slot_tiled = jnp.where(hit, 1.0, 0.0)
    slot_own = jnp.where(iota((ports, LANES), 1) // elems == me % group, slot_tiled, 0.0)
    r8 = iota((8, ports), 0)
    params = jnp.where(
        r8 == TAGS,
        iota((8, ports), 1).astype(F32),
        jnp.where(
            r8 == TAGS + 1,
            again,
            jnp.where(r8 == TAGS + 2, cgain, jnp.where(r8 == TAGS + 3, prev, flux)),
        ),
    )
    p1 = params.astype(BF16).astype(F32)
    p2 = (params - p1).astype(BF16).astype(F32)
    parts = dot(jnp.concatenate([p1, p2, params - p1 - p2], axis=0).astype(BF16), slot_own.astype(BF16))
    par = (parts[:8] + parts[8:16]) + parts[16:24]
    k8 = iota((8, LANES), 0)
    tags = jnp.where(k8 == 0, dest, jnp.where(k8 == 1, port // ports, port % ports))
    mine_at = c * zn + z
    unit[mine_at, :STEPS, :] = shifted[:STEPS, :]
    unit[mine_at, STEPS:, :] = jnp.where(k8 < TAGS, tags.astype(F32), par)

    def remote(ref_from, ref_to, send, recv, to_sub, to_row):
        return pltpu.make_async_remote_copy(
            src_ref=ref_from, dst_ref=ref_to, send_sem=send, recv_sem=recv,
            device_id=(to_sub, to_row), device_id_type=MESH,
        )

    def unit_copy(zz, at, target):
        ref = unit.at[c * zn + zz]
        return remote(ref, ref, unit_sem.at[0], unit_sem.at[1 + at], s, target)

    def line_copy(b, target):
        return remote(gath.at[b], gath.at[b], line_sem.at[0], line_recv.at[b], s, target)

    def pass_copy(b):
        return remote(gath.at[b], gath.at[b], line_sem.at[1], line_recv.at[b], s, partner)

    def send_subs(zz):
        for j in range(1, subs):
            remote(
                unit.at[c * zn + zz], got_units.at[c, j - 1, zz], sub_sem.at[0], sub_sem.at[1], s ^ j, me
            ).start()

    def both_copy(cc):
        return remote(got_units.at[cc], got_units.at[cc], both_sem.at[0], both_sem.at[1], s, partner)

    def elem_copy(b, kind, target):
        return remote(elem.at[b], elem.at[b], elem_sem.at[0], elem_sem.at[1 + kind], s, target)

    def fst_copy(target):
        return remote(fst.at[me], fst.at[me], fst_sem.at[0], fst_sem.at[1], s, target)

    def sent(ref, sem):
        remote(ref, ref, sem, sem, s, partner).wait_send()

    def arrived(ref, sem):
        remote(ref, ref, sem, sem, s, partner).wait_recv()

    src_copy.wait()
    pl.semaphore_wait(barrier, rows - 1 + len(bits))

    def tell_subs(k):
        for bit in bits:
            pl.semaphore_signal(sub_in.at[k], inc=1, device_id=(s ^ bit, me), device_id_type=MESH)

    tell_subs(0)

    for j in range(1, zn):
        unit_copy(z, z, lax.rem(z + j, zn) * 2 + c).start()
    unit_copy(z, zn, partner).start()

    for dist in [1] + list(range(zn - 1, 1, -1)):
        up, down = z + dist, z - dist

        @pl.when(jnp.logical_and(up < zn, jnp.logical_or(dist != 2, up != zn - 1)))
        def _():
            line_copy(me, up * 2 + c).start()

        @pl.when(jnp.logical_and(down >= 0, jnp.logical_or(dist != 2, down != 0)))
        def _():
            line_copy(me, down * 2 + c).start()

    pass_copy(me).start()
    lower, upper = z == 1, z == zn - 2
    relays = jnp.logical_or(lower, upper)
    skips = jnp.logical_or(z == 2, z == zn - 3)
    znear = jnp.where(z < zn // 2, z + 1, z - 1)

    acc[...] = jnp.zeros_like(acc)
    hacc[...] = jnp.zeros_like(hacc)

    def split_block(b, carry):
        cols = pl.ds(pl.multiple_of(b * slice_len, LANES), slice_len)
        high, low = hi_lo(m32[:, cols])
        m2[:ports, cols] = high
        m2[ports:, cols] = low
        at_ports = pl.ds(pl.multiple_of(b * ports, LANES), ports)
        mp2[:ports, at_ports] = high[:, :ports]
        mp2[ports:, at_ports] = low[:, :ports]
        return carry

    def use_sources(b):
        cols = pl.ds(pl.multiple_of(b * slice_len, LANES), slice_len)
        acc[...] += dot(stack_hi_lo(gath[b]), m2[:, cols], NT)

    for h in range(HALVES):
        inv_copy(h).wait()
        lax.fori_loop(h * rows // HALVES, (h + 1) * rows // HALVES, split_block, 0)
    use_sources(me)

    for k in range(len(bits) - 1):
        pl.semaphore_wait(sub_in.at[k], len(bits))
        if k < len(bits) - 2:
            tell_subs(k + 1)
    send_subs(z)
    toward = jnp.where(z < zn // 2, 1, zn - 1)
    for j in range(1, zn):
        zz = lax.rem(z + j * toward, zn)
        unit_copy(zz, zz, partner).wait_recv()
        unit_copy(zz, zn, partner).start()
        send_subs(zz)

    def other_chips(lo, hi, act):
        def body(q, carry):
            i = jnp.where(jnp.logical_or(z == 0, z == zn - 1), turns - 1 - q, q)
            zb = jnp.where(i % 2 == 0, z - i // 2 - 1, z + i // 2 + 1)

            @pl.when(jnp.logical_and(jnp.logical_and(zb >= 0, zb < zn), zb != znear))
            def _():
                act(zb)

            return carry

        lax.fori_loop(lo, hi, body, 0)

    def take(zb):
        line_copy(zb * 2 + c, partner).wait_recv()
        pass_copy(zb * 2 + c).start()

    def use_own(zb):
        use_sources(zb * 2 + c)

    def use_passed(zb):
        pass_copy(zb * 2 + 1 - c).wait_recv()
        use_sources(zb * 2 + 1 - c)

    use_passed(z)
    line_copy(znear * 2 + c, partner).wait_recv()

    @pl.when(relays)
    def _():
        line_copy(znear * 2 + c, jnp.where(lower, z - 1, z + 1) * 2 + c).start()

    pass_copy(znear * 2 + c).start()
    use_own(znear)
    use_passed(znear)

    arrived(unit.at[pl.ds(0, zn)], unit_sem.at[1 + zn])
    all_par = jnp.concatenate(
        [
            sum(unit[(h * group + i) % 2 * zn + (h * group + i) // 2, STEPS:, :] for i in range(group))
            for h in range(halves)
        ],
        axis=1,
    )
    slots_all = all_par[TAGS : TAGS + 1, :]
    at_slot = iota((ports, total), 0).astype(F32) == slots_all
    owner_of = iota((ports, total), 1) // elems
    pick = None
    for r in range(rows):
        choose = jnp.where(jnp.logical_and(at_slot, owner_of == r), 1.0, 0.0).astype(BF16)
        term = dot(mp2[:, r * ports : (r + 1) * ports], choose)
        pick = term if pick is None else pick + term
    x2[...] = pick.astype(BF16)
    slot_cols = jnp.transpose(slot_tiled)[:elems].astype(BF16)
    elem[me] = dot(slot_cols, x2[:ports, :]) + dot(slot_cols, x2[ports:, :])
    for j in range(1, zn):
        elem_copy(me, 0, lax.rem(z + j, zn) * 2 + c).start()
    elem_copy(me, 1, partner).start()

    arrived(got_units.at[c], sub_sem.at[1])
    both_copy(c).start()

    def use_records(cc):
        blocks = [(x, zz) for zz in range(zn) for x in range(peers)]
        values = jnp.concatenate([got_units[cc, x, zz, :STEPS, :] for x, zz in blocks], axis=1)
        tag = jnp.concatenate([got_units[cc, x, zz, STEPS:, :] for x, zz in blocks], axis=1)
        owner = jnp.where(tag[0:1, :] == s.astype(F32), tag[1:2, :], -1.0)
        spot = tag[2:3, :]
        wide = values.shape[1]
        land = jnp.where(iota((ports, wide), 0).astype(F32) == spot, 1.0, 0.0).astype(BF16)
        high, low = hi_lo(values)
        wide_owner = jnp.broadcast_to(owner, (STEPS, wide))
        split = []
        for r in range(rows):
            mine = jnp.where(wide_owner == float(r), 1.0, 0.0).astype(BF16)
            split += [high * mine, low * mine]
        hacc[...] += dot(jnp.concatenate(split, axis=0), land, NT)

    use_records(c)

    def take_use(zb):
        take(zb)
        use_own(zb)

    other_chips(0, 2, take_use)
    both_copy(1 - c).wait_recv()
    use_records(1 - c)
    other_chips(2, turns, take_use)
    other_chips(0, turns, use_passed)

    landed = jnp.concatenate(
        [
            hacc[2 * r * STEPS : (2 * r + 1) * STEPS, :] + hacc[(2 * r + 1) * STEPS : (2 * r + 2) * STEPS, :]
            for r in range(rows)
        ],
        axis=1,
    )
    first = four_terms(acc[...] - dot(stack_hi_lo(landed), mp2[...], NT))
    mine = dot(stack_hi_lo(first), slot_own.astype(BF16))
    fst[me] = mine[:STEPS] + mine[STEPS:]
    for j in range(1, rows):
        fst_copy(lax.rem(me + j, rows)).start()

    arrived(elem.at[pl.ds(0, zn - 1)], elem_sem.at[1])
    for j in range(1, zn):
        elem_copy(lax.rem(z + j, zn) * 2 + c, 1, partner).start()
    arrived(elem.at[pl.ds(0, zn)], elem_sem.at[2])

    w = elem[...].reshape(total, total)
    self_row = jnp.sum(jnp.where(iota((total, total), 0) == iota((total, total), 1), w, 0.0), axis=0, keepdims=True)
    w_hi, w_lo = hi_lo(jnp.transpose(w))
    wc[:, :total] = w_hi
    wc[:, total:] = w_lo

    full = (8, total)
    is_arrest = iota(full, 1) % elems < arrests
    rowp = lambda i: jnp.broadcast_to(all_par[TAGS + i : TAGS + i + 1, :], full)
    arrest_gain = jnp.where(is_arrest, rowp(1), 0.0)
    core_gain = jnp.where(is_arrest, 0.0, rowp(2))
    elem_self = jnp.broadcast_to(self_row, full)
    volts0 = rowp(3)
    flux0 = rowp(4)
    put = jnp.where(jnp.logical_and(at_slot, owner_of == me), 1.0, 0.0).astype(BF16)
    here = dot(jnp.ones((8, total), BF16), put, NT)[0:1]

    sent(got_units.at[c], sub_sem.at[0])
    sent(got_units.at[c], both_sem.at[0])
    sent(gath.at[pl.ds(0, zn)], line_sem.at[1])
    line_sends = zn - 1 + relays.astype(jnp.int32) - skips.astype(jnp.int32)
    for n in range(zn - 2, zn + 1):
        @pl.when(line_sends == n)
        def _():
            sent(gath.at[pl.ds(0, n)], line_sem.at[0])

    sent(unit.at[pl.ds(0, 2 * zn - 1)], unit_sem.at[0])
    sent(elem.at[pl.ds(0, 2 * zn - 1)], elem_sem.at[0])
    arrived(fst.at[pl.ds(0, rows - 1)], fst_sem.at[1])
    fall[...] = jnp.concatenate(
        [sum(fst[h * group + i] for i in range(group)) for h in range(halves)], axis=1
    )

    def advance(t, carry):
        voltage, flux_now = carry
        first_now = jnp.broadcast_to(fall[pl.ds(t, 1), :], full)
        iterate = voltage
        for newton_pass in range(NEWTON):
            linked = flux_now + half_step * (iterate + voltage)
            ratio = iterate * (1.0 / knee_volts)
            rr = ratio * ratio
            ll = linked * linked
            current = arrest_gain * (iterate * (1.0 + rr)) + core_gain * (linked * (1.0 + cubic_term * ll))
            slope = arrest_gain * (1.0 + 3.0 * rr) + core_gain * (half_step + (half_step * 3.0 * cubic_term) * ll)
            recip = 1.0 / (1.0 + elem_self * slope)
            got = dot(stack_hi_lo(current), wc[...])
            coupled = got[:8, :total] + got[8:, :total] + got[:8, total:]
            iterate = iterate - (iterate - first_now + coupled) * recip
        vo[pl.ds(t, 1), :] = iterate[0:1]
        cu[pl.ds(t, 1), :] = current[0:1]
        return iterate, flux_now + half_step * (iterate + voltage)

    lax.fori_loop(0, STEPS, advance, (volts0, flux0), unroll=4)

    reach = four_terms(dot(stack_hi_lo(cu[...]), x2[...], NT))
    placed = dot(stack_hi_lo(vo[...]), put, NT)
    stacked = jnp.where(here > 0.5, placed[:STEPS] + placed[STEPS:], first - reach)
    out[:STEPS, :] = stacked
    summed = jnp.sum(stacked, axis=0, keepdims=True)
    last_flux = flux + half_step * (prev + 2.0 * summed - stacked[STEPS - 1 : STEPS])
    out[STEPS:, :] = jnp.broadcast_to(last_flux, (8, ports))
    sent(fst.at[pl.ds(0, rows - 1)], fst_sem.at[0])


def give(both, volts, last_flux):
    volts[0] = both[:STEPS, :]
    last_flux[...] = both[STEPS : STEPS + 1, :]


def on_device(subs, rows, *args):
    inverse, sources = args[0], args[1]
    ports = inverse.shape[1]
    order = inverse.shape[2]
    slice_len = sources.shape[2]
    arrests, cores = args[10].shape[1], args[11].shape[1]
    elems = arrests + cores
    total = rows * elems
    zn = rows // 2
    vmem = pl.BlockSpec(memory_space=pltpu.VMEM)
    hbm = pl.BlockSpec(memory_space=pl.ANY)
    dma = pltpu.SemaphoreType.DMA
    small = args[2:]
    both = pl.pallas_call(
        functools.partial(kernel, subs, rows, ports, slice_len, arrests, cores, len(small)),
        out_shape=pltpu.VMEM((STEPS + 8, ports), F32),
        in_specs=[hbm] * len(args),
        out_specs=vmem,
        scratch_shapes=[
            pltpu.VMEM(small[0].shape, F32),
            pltpu.VMEM((8, LANES), jnp.int32),
            pltpu.VMEM((8, LANES), F32),
            pltpu.VMEM((2, 1, arrests), jnp.int32),
            pltpu.VMEM((ports, order), F32),
            pltpu.VMEM((2 * ports, order), BF16),
            pltpu.VMEM((2 * ports, rows * ports), BF16),
            pltpu.VMEM((rows, STEPS, slice_len), F32),
            pltpu.VMEM((2 * zn, STEPS + 8, LANES), F32),
            pltpu.VMEM((2, subs - 1, zn, STEPS + 8, LANES), F32),
            pltpu.VMEM((rows, elems, total), F32),
            pltpu.VMEM((rows, STEPS, LANES), F32),
            pltpu.VMEM((2 * ports, total), BF16),
            pltpu.VMEM((total, 2 * total), BF16),
            pltpu.VMEM((STEPS, total), F32),
            pltpu.VMEM((STEPS, total), F32),
            pltpu.VMEM((STEPS, total), F32),
            pltpu.VMEM((2 * STEPS, 2 * ports), F32),
            pltpu.VMEM((2 * STEPS * rows, ports), F32),
            dma((5,)),
            dma((HALVES,)),
            dma((2,)),
            dma((rows,)),
            dma((zn + 2,)),
            dma((2,)),
            pltpu.SemaphoreType.REGULAR((max((subs - 1).bit_length() - 1, 1),)),
            dma((2,)),
            dma((3,)),
            dma((2,)),
        ],
        compiler_params=pltpu.CompilerParams(collective_id=0, has_side_effects=True),
        name="window",
    )(*args)
    return pl.pallas_call(
        give,
        out_shape=(
            jax.ShapeDtypeStruct((1, STEPS, ports), F32),
            jax.ShapeDtypeStruct((1, ports), F32),
        ),
        in_specs=[vmem],
        out_specs=(vmem, vmem),
        name="give",
    )(pltpu.with_memory_space_constraint(both, pltpu.VMEM))


def solution(mesh):
    subs, rows = mesh.shape["sub"], mesh.shape["row"]
    in_specs = (
        P("sub", "row", None),
        P("sub", None, "row"),
        P("sub", None, "row"),
    ) + (P("sub", "row"),) * 9
    out_specs = (P("sub", None, "row"), P("sub", "row"))
    return jax.shard_map(
        functools.partial(on_device, subs, rows),
        mesh=mesh, in_specs=in_specs, out_specs=out_specs, check_vma=False,
    )
```

```python
import functools

import jax
import jax.numpy as jnp
from jax import lax
from jax.experimental import pallas as pl
from jax.experimental.pallas import tpu as pltpu
from jax.sharding import PartitionSpec as P

STEPS = 16
HISTORY = 32
NEWTON = 2
LANES = 128
TAGS = 3
HALVES = 2
PART = STEPS // 2

half_step = 0.25
knee_volts = 1.5
cubic_term = 0.25

F32 = jnp.float32
BF16 = jnp.bfloat16
MESH = pl.DeviceIdType.MESH
NN = (((1,), (0,)), ((), ()))
NT = (((1,), (1,)), ((), ()))
HIGHEST = lax.Precision.HIGHEST


def iota(shape, axis):
    return lax.broadcasted_iota(jnp.int32, shape, axis)


def hi_lo(x):
    high = x.astype(BF16)
    return high, (x - high.astype(F32)).astype(BF16)


def stack_hi_lo(x):
    return jnp.concatenate(hi_lo(x), axis=0)


def dot(a, b, dims=NN):
    return lax.dot_general(a, b, dims, preferred_element_type=F32)


def four_terms(r):
    n, m = r.shape[0] // 2, r.shape[1] // 2
    return (r[:n, :m] + r[n:, :m]) + (r[:n, m:] + r[n:, m:])


def kernel(
    subs, rows, ports, slice_len, arrests, cores, n_small,
    inv, src, *refs,
):
    small_hbm, refs = refs[:n_small], refs[n_small:]
    (
        out, hist, tags_i, gains, slots, m32, m2, mp2, gath, unit, got_units, elem, fst,
        x2, wc, fall, vo, cu, acc, hacc,
        small_sem, inv_sem, line_sem, line_recv, unit_sem, sub_sem, sub_in, both_sem, elem_sem, fst_sem,
    ) = refs
    s = lax.axis_index("sub")
    me = lax.axis_index("row")
    z, c = me // 2, me % 2
    zn = rows // 2
    partner = z * 2 + (1 - c)
    elems = arrests + cores
    group = LANES // elems
    total = rows * elems
    halves = total // LANES
    peers = subs - 1
    turns = 2 * (zn - 1)

    barrier = pltpu.get_barrier_semaphore()
    for j in range(1, rows):
        pl.semaphore_signal(barrier, inc=1, device_id=(s, lax.rem(me + j, rows)), device_id_type=MESH)
    bits = [1 << k for k in range((subs - 1).bit_length())]
    for bit in bits:
        pl.semaphore_signal(barrier, inc=1, device_id=(s ^ bit, me), device_id_type=MESH)

    ints, floats = small_hbm[1:4], small_hbm[4:8]
    pltpu.make_async_copy(small_hbm[0], hist, small_sem.at[0]).start()
    for i, ref in enumerate(ints):
        pltpu.make_async_copy(ref, tags_i.at[pl.ds(i, 1)], small_sem.at[1]).start()
    for i, ref in enumerate(floats):
        pltpu.make_async_copy(ref, gains.at[pl.ds(i, 1)], small_sem.at[2]).start()
    for i, ref in enumerate(small_hbm[8:]):
        pltpu.make_async_copy(ref, slots.at[i], small_sem.at[3]).start()
    src_copy = pltpu.make_async_copy(src.at[0], gath.at[me], small_sem.at[4])
    src_copy.start()

    def wait_all(ref, sem):
        pltpu.make_async_copy(ref, ref, sem).wait()

    wait_all(hist, small_sem.at[0])
    wait_all(tags_i.at[pl.ds(0, len(ints))], small_sem.at[1])
    wait_all(gains.at[pl.ds(0, len(floats))], small_sem.at[2])
    wait_all(slots, small_sem.at[3])
    dest, port, delay = (tags_i[i : i + 1, :] for i in range(len(ints)))
    prev, flux, again, cgain = (gains[i : i + 1, :] for i in range(len(floats)))

    span = m32.shape[1] // HALVES

    def inv_copy(h):
        cols = pl.ds(h * span, span)
        return pltpu.make_async_copy(inv.at[0, :, cols], m32.at[:, cols], inv_sem.at[h])

    for h in range(HALVES):
        inv_copy(h).start()

    shifted = hist[0]
    shift = HISTORY - delay
    bit = 1
    while bit <= HISTORY - STEPS:
        moved = pltpu.roll(shifted, HISTORY - bit, 0)
        shifted = jnp.where((shift // bit) % 2 == 1, moved, shifted)
        bit *= 2

    lane16a, row16a = iota((arrests, LANES), 1), iota((arrests, LANES), 0)
    lane16c, row16c = iota((cores, LANES), 1), iota((cores, LANES), 0)
    put_a = jnp.where(lane16a % elems == row16a, 1.0, 0.0).astype(BF16)
    put_c = jnp.where(lane16c % elems == row16c + arrests, 1.0, 0.0).astype(BF16)
    slot_a = jnp.broadcast_to(slots[0].astype(F32), (8, arrests)).astype(BF16)
    slot_c = jnp.broadcast_to(slots[1].astype(F32), (8, cores)).astype(BF16)
    slot_row = (dot(slot_a, put_a) + dot(slot_c, put_c))[0:1, :]
    hit = iota((ports, LANES), 0).astype(F32) == slot_row
    slot_tiled = jnp.where(hit, 1.0, 0.0)
    slot_own = jnp.where(iota((ports, LANES), 1) // elems == me % group, slot_tiled, 0.0)
    r8 = iota((8, ports), 0)
    params = jnp.where(
        r8 == TAGS,
        iota((8, ports), 1).astype(F32),
        jnp.where(
            r8 == TAGS + 1,
            again,
            jnp.where(r8 == TAGS + 2, cgain, jnp.where(r8 == TAGS + 3, prev, flux)),
        ),
    )
    p1 = params.astype(BF16).astype(F32)
    p2 = (params - p1).astype(BF16).astype(F32)
    parts = dot(jnp.concatenate([p1, p2, params - p1 - p2], axis=0).astype(BF16), slot_own.astype(BF16))
    par = (parts[:8] + parts[8:16]) + parts[16:24]
    k8 = iota((8, LANES), 0)
    tags = jnp.where(k8 == 0, dest, jnp.where(k8 == 1, port // ports, port % ports))
    mine_at = c * zn + z
    unit[mine_at, :STEPS, :] = shifted[:STEPS, :]
    unit[mine_at, STEPS:, :] = jnp.where(k8 < TAGS, tags.astype(F32), par)

    def remote(ref_from, ref_to, send, recv, to_sub, to_row):
        return pltpu.make_async_remote_copy(
            src_ref=ref_from, dst_ref=ref_to, send_sem=send, recv_sem=recv,
            device_id=(to_sub, to_row), device_id_type=MESH,
        )

    def unit_copy(zz, at, target):
        ref = unit.at[c * zn + zz]
        return remote(ref, ref, unit_sem.at[0], unit_sem.at[1 + at], s, target)

    def line_copy(b, target):
        return remote(gath.at[b], gath.at[b], line_sem.at[0], line_recv.at[b], s, target)

    def part_copy(h, b, target):
        ref = gath.at[b, pl.ds(h * PART, PART)]
        return remote(ref, ref, line_sem.at[0], line_recv.at[b if h == 0 else rows], s, target)

    def relay_copy(h, b, target):
        ref = gath.at[b, pl.ds(h * PART, PART)]
        return remote(ref, ref, line_sem.at[0], line_recv.at[b], s, target)

    def pass_copy(b):
        return remote(gath.at[b], gath.at[b], line_sem.at[1], line_recv.at[b], s, partner)

    def send_subs(zz):
        for j in range(1, subs):
            remote(
                unit.at[c * zn + zz], got_units.at[c, j - 1, zz], sub_sem.at[0], sub_sem.at[1], s ^ j, me
            ).start()

    def both_copy(cc):
        return remote(got_units.at[cc], got_units.at[cc], both_sem.at[0], both_sem.at[1], s, partner)

    def elem_copy(b, kind, target):
        return remote(elem.at[b], elem.at[b], elem_sem.at[0], elem_sem.at[1 + kind], s, target)

    def fst_copy(target):
        return remote(fst.at[me], fst.at[me], fst_sem.at[0], fst_sem.at[1], s, target)

    def sent(ref, sem):
        remote(ref, ref, sem, sem, s, partner).wait_send()

    def arrived(ref, sem):
        remote(ref, ref, sem, sem, s, partner).wait_recv()

    src_copy.wait()
    pl.semaphore_wait(barrier, rows - 1 + len(bits))

    def tell_subs(k):
        for bit in bits:
            pl.semaphore_signal(sub_in.at[k], inc=1, device_id=(s ^ bit, me), device_id_type=MESH)

    tell_subs(0)

    for j in range(1, zn):
        unit_copy(z, z, lax.rem(z + j, zn) * 2 + c).start()
    unit_copy(z, zn, partner).start()

    def send_near(target, relayed):
        @pl.when(relayed)
        def _():
            for h in range(2):
                part_copy(h, me, target).start()

        @pl.when(jnp.logical_not(relayed))
        def _():
            line_copy(me, target).start()

    for dist in [1] + list(range(zn - 1, 1, -1)):
        up, down = z + dist, z - dist

        @pl.when(jnp.logical_and(up < zn, jnp.logical_or(dist != 2, up != zn - 1)))
        def _():
            if dist == 1:
                send_near(up * 2 + c, up == zn - 2)
            else:
                line_copy(me, up * 2 + c).start()

        @pl.when(jnp.logical_and(down >= 0, jnp.logical_or(dist != 2, down != 0)))
        def _():
            if dist == 1:
                send_near(down * 2 + c, down == 1)
            else:
                line_copy(me, down * 2 + c).start()

    pass_copy(me).start()
    lower, upper = z == 1, z == zn - 2
    relays = jnp.logical_or(lower, upper)
    skips = jnp.logical_or(z == 2, z == zn - 3)
    znear = jnp.where(z < zn // 2, z + 1, z - 1)

    hacc[...] = jnp.zeros_like(hacc)

    def split_block(b, carry):
        cols = pl.ds(pl.multiple_of(b * slice_len, LANES), slice_len)
        high, low = hi_lo(m32[:, cols])
        m2[:ports, cols] = high
        m2[ports:, cols] = low
        at_ports = pl.ds(pl.multiple_of(b * ports, LANES), ports)
        mp2[:ports, at_ports] = high[:, :ports]
        mp2[ports:, at_ports] = low[:, :ports]
        return carry

    def columns(b, count):
        return pl.ds(pl.multiple_of(b * slice_len, LANES), count * slice_len)

    def use_sources(b):
        acc[...] += dot(stack_hi_lo(gath[b]), m2[:, columns(b, 1)], NT)

    for h in range(HALVES):
        inv_copy(h).wait()
        lax.fori_loop(h * rows // HALVES, (h + 1) * rows // HALVES, split_block, 0)
    pass_copy(partner).wait_recv()
    home = jnp.concatenate([gath[z * 2], gath[z * 2 + 1]], axis=1)
    acc[...] = dot(stack_hi_lo(home), m2[:, columns(z * 2, 2)], NT)

    for k in range(len(bits) - 1):
        pl.semaphore_wait(sub_in.at[k], len(bits))
        if k < len(bits) - 2:
            tell_subs(k + 1)
    send_subs(z)
    toward = jnp.where(z < zn // 2, 1, zn - 1)
    for j in range(1, zn):
        zz = lax.rem(z + j * toward, zn)
        unit_copy(zz, zz, partner).wait_recv()
        unit_copy(zz, zn, partner).start()
        send_subs(zz)

    def other_chips(lo, hi, act):
        def body(q, carry):
            i = jnp.where(jnp.logical_or(z == 0, z == zn - 1), turns - 1 - q, q)
            zb = jnp.where(i % 2 == 0, z - i // 2 - 1, z + i // 2 + 1)

            @pl.when(jnp.logical_and(jnp.logical_and(zb >= 0, zb < zn), zb != znear))
            def _():
                act(zb)

            return carry

        lax.fori_loop(lo, hi, body, 0)

    def take(zb):
        line_copy(zb * 2 + c, partner).wait_recv()
        pass_copy(zb * 2 + c).start()

    def use_own(zb):
        use_sources(zb * 2 + c)

    def use_passed(zb):
        pass_copy(zb * 2 + 1 - c).wait_recv()
        use_sources(zb * 2 + 1 - c)

    near = znear * 2 + c
    outer = jnp.where(lower, z - 1, z + 1) * 2 + c

    @pl.when(relays)
    def _():
        for h in range(2):
            part_copy(h, near, partner).wait_recv()
            relay_copy(h, near, outer).start()

    @pl.when(jnp.logical_not(relays))
    def _():
        line_copy(near, partner).wait_recv()

    pass_copy(znear * 2 + c).start()
    use_own(znear)
    use_passed(znear)

    arrived(unit.at[pl.ds(0, zn)], unit_sem.at[1 + zn])
    all_par = jnp.concatenate(
        [
            sum(unit[(h * group + i) % 2 * zn + (h * group + i) // 2, STEPS:, :] for i in range(group))
            for h in range(halves)
        ],
        axis=1,
    )
    slots_all = all_par[TAGS : TAGS + 1, :]
    at_slot = iota((ports, total), 0).astype(F32) == slots_all
    owner_of = iota((ports, total), 1) // elems
    choose = [
        jnp.where(jnp.logical_and(at_slot, owner_of == r), 1.0, 0.0).astype(BF16) for r in range(rows)
    ]
    x2[...] = dot(mp2[...], jnp.concatenate(choose, axis=0)).astype(BF16)
    slot_cols = jnp.transpose(slot_tiled)[:elems].astype(BF16)
    elem[me] = dot(slot_cols, x2[:ports, :]) + dot(slot_cols, x2[ports:, :])
    for j in range(1, zn):
        elem_copy(me, 0, lax.rem(z + j, zn) * 2 + c).start()
    elem_copy(me, 1, partner).start()

    def take_use(zb):
        take(zb)
        use_own(zb)

    other_chips(0, 2, take_use)
    arrived(got_units.at[c], sub_sem.at[1])
    both_copy(c).start()

    def use_records(cc):
        blocks = [(x, zz) for zz in range(zn) for x in range(peers)]
        values = jnp.concatenate([got_units[cc, x, zz, :STEPS, :] for x, zz in blocks], axis=1)
        tag = jnp.concatenate([got_units[cc, x, zz, STEPS:, :] for x, zz in blocks], axis=1)
        owner = jnp.where(tag[0:1, :] == s.astype(F32), tag[1:2, :], -1.0)
        spot = tag[2:3, :]
        wide = values.shape[1]
        land = jnp.where(iota((ports, wide), 0).astype(F32) == spot, 1.0, 0.0).astype(BF16)
        high, low = hi_lo(values)
        wide_owner = jnp.broadcast_to(owner, (STEPS, wide))
        split = []
        for r in range(rows):
            mine = jnp.where(wide_owner == float(r), 1.0, 0.0).astype(BF16)
            split += [high * mine, low * mine]
        hacc[...] += dot(jnp.concatenate(split, axis=0), land, NT)

    use_records(c)
    other_chips(2, turns, take_use)
    other_chips(0, 2, use_passed)
    both_copy(1 - c).wait_recv()
    use_records(1 - c)
    other_chips(2, turns, use_passed)

    landed = jnp.concatenate(
        [
            hacc[2 * r * STEPS : (2 * r + 1) * STEPS, :] + hacc[(2 * r + 1) * STEPS : (2 * r + 2) * STEPS, :]
            for r in range(rows)
        ],
        axis=1,
    )
    first = four_terms(acc[...] - dot(stack_hi_lo(landed), mp2[...], NT))
    mine = dot(stack_hi_lo(first), slot_own.astype(BF16))
    fst[me] = mine[:STEPS] + mine[STEPS:]
    for j in range(1, rows):
        fst_copy(lax.rem(me + j, rows)).start()

    arrived(elem.at[pl.ds(0, zn - 1)], elem_sem.at[1])
    for j in range(1, zn):
        elem_copy(lax.rem(z + j, zn) * 2 + c, 1, partner).start()
    arrived(elem.at[pl.ds(0, zn)], elem_sem.at[2])

    w = elem[...].reshape(total, total)
    self_row = jnp.sum(jnp.where(iota((total, total), 0) == iota((total, total), 1), w, 0.0), axis=0, keepdims=True)
    w_hi, w_lo = hi_lo(jnp.transpose(w))
    wc[:, :total] = w_hi
    wc[:, total:] = w_lo

    full = (8, total)
    is_arrest = iota(full, 1) % elems < arrests
    rowp = lambda i: jnp.broadcast_to(all_par[TAGS + i : TAGS + i + 1, :], full)
    arrest_gain = jnp.where(is_arrest, rowp(1), 0.0)
    core_gain = jnp.where(is_arrest, 0.0, rowp(2))
    elem_self = jnp.broadcast_to(self_row, full)
    volts0 = rowp(3)
    flux0 = rowp(4)
    put = jnp.where(jnp.logical_and(at_slot, owner_of == me), 1.0, 0.0).astype(BF16)
    here = dot(jnp.ones((8, total), BF16), put, NT)[0:1]

    sent(got_units.at[c], sub_sem.at[0])
    sent(got_units.at[c], both_sem.at[0])
    sent(gath.at[pl.ds(0, zn)], line_sem.at[1])
    line_sends = zn - 1 + relays.astype(jnp.int32) - skips.astype(jnp.int32)
    for n in range(zn - 2, zn + 1):
        @pl.when(line_sends == n)
        def _():
            sent(gath.at[pl.ds(0, n)], line_sem.at[0])

    sent(unit.at[pl.ds(0, 2 * zn - 1)], unit_sem.at[0])
    sent(elem.at[pl.ds(0, 2 * zn - 1)], elem_sem.at[0])
    arrived(fst.at[pl.ds(0, rows - 1)], fst_sem.at[1])
    fall[...] = jnp.concatenate(
        [sum(fst[h * group + i] for i in range(group)) for h in range(halves)], axis=1
    )

    def advance(t, carry):
        voltage, flux_now = carry
        first_now = jnp.broadcast_to(fall[pl.ds(t, 1), :], full)
        iterate = voltage
        for newton_pass in range(NEWTON):
            linked = flux_now + half_step * (iterate + voltage)
            ratio = iterate * (1.0 / knee_volts)
            rr = ratio * ratio
            ll = linked * linked
            current = arrest_gain * (iterate * (1.0 + rr)) + core_gain * (linked * (1.0 + cubic_term * ll))
            slope = arrest_gain * (1.0 + 3.0 * rr) + core_gain * (half_step + (half_step * 3.0 * cubic_term) * ll)
            recip = 1.0 / (1.0 + elem_self * slope)
            got = dot(stack_hi_lo(current), wc[...])
            settled = iterate - (iterate - first_now) * recip
            coupled = (got[:8, :total] + got[8:, :total]) + got[:8, total:]
            iterate = settled - coupled * recip
        vo[pl.ds(t, 1), :] = iterate[0:1]
        cu[pl.ds(t, 1), :] = current[0:1]
        return iterate, flux_now + half_step * (iterate + voltage)

    lax.fori_loop(0, STEPS, advance, (volts0, flux0), unroll=8)

    reach = four_terms(dot(stack_hi_lo(cu[...]), x2[...], NT))
    placed = dot(stack_hi_lo(vo[...]), put, NT)
    stacked = jnp.where(here > 0.5, placed[:STEPS] + placed[STEPS:], first - reach)
    out[:STEPS, :] = stacked
    summed = jnp.sum(stacked, axis=0, keepdims=True)
    last_flux = flux + half_step * (prev + 2.0 * summed - stacked[STEPS - 1 : STEPS])
    out[STEPS:, :] = jnp.broadcast_to(last_flux, (8, ports))
    sent(fst.at[pl.ds(0, rows - 1)], fst_sem.at[0])


def give(both, volts, last_flux):
    volts[0] = both[:STEPS, :]
    last_flux[...] = both[STEPS : STEPS + 1, :]


def on_device(subs, rows, *args):
    inverse, sources = args[0], args[1]
    ports = inverse.shape[1]
    order = inverse.shape[2]
    slice_len = sources.shape[2]
    arrests, cores = args[10].shape[1], args[11].shape[1]
    elems = arrests + cores
    total = rows * elems
    zn = rows // 2
    vmem = pl.BlockSpec(memory_space=pltpu.VMEM)
    hbm = pl.BlockSpec(memory_space=pl.ANY)
    dma = pltpu.SemaphoreType.DMA
    small = args[2:]
    both = pl.pallas_call(
        functools.partial(kernel, subs, rows, ports, slice_len, arrests, cores, len(small)),
        out_shape=pltpu.VMEM((STEPS + 8, ports), F32),
        in_specs=[hbm] * len(args),
        out_specs=vmem,
        scratch_shapes=[
            pltpu.VMEM(small[0].shape, F32),
            pltpu.VMEM((8, LANES), jnp.int32),
            pltpu.VMEM((8, LANES), F32),
            pltpu.VMEM((2, 1, arrests), jnp.int32),
            pltpu.VMEM((ports, order), F32),
            pltpu.VMEM((2 * ports, order), BF16),
            pltpu.VMEM((2 * ports, rows * ports), BF16),
            pltpu.VMEM((rows, STEPS, slice_len), F32),
            pltpu.VMEM((2 * zn, STEPS + 8, LANES), F32),
            pltpu.VMEM((2, subs - 1, zn, STEPS + 8, LANES), F32),
            pltpu.VMEM((rows, elems, total), F32),
            pltpu.VMEM((rows, STEPS, LANES), F32),
            pltpu.VMEM((2 * ports, total), BF16),
            pltpu.VMEM((total, 2 * total), BF16),
            pltpu.VMEM((STEPS, total), F32),
            pltpu.VMEM((STEPS, total), F32),
            pltpu.VMEM((STEPS, total), F32),
            pltpu.VMEM((2 * STEPS, 2 * ports), F32),
            pltpu.VMEM((2 * STEPS * rows, ports), F32),
            dma((5,)),
            dma((HALVES,)),
            dma((2,)),
            dma((rows + 1,)),
            dma((zn + 2,)),
            dma((2,)),
            pltpu.SemaphoreType.REGULAR((max((subs - 1).bit_length() - 1, 1),)),
            dma((2,)),
            dma((3,)),
            dma((2,)),
        ],
        compiler_params=pltpu.CompilerParams(collective_id=0, has_side_effects=True),
        name="window",
    )(*args)
    return pl.pallas_call(
        give,
        out_shape=(
            jax.ShapeDtypeStruct((1, STEPS, ports), F32),
            jax.ShapeDtypeStruct((1, ports), F32),
        ),
        in_specs=[vmem],
        out_specs=(vmem, vmem),
        name="give",
    )(pltpu.with_memory_space_constraint(both, pltpu.VMEM))


def solution(mesh):
    subs, rows = mesh.shape["sub"], mesh.shape["row"]
    in_specs = (
        P("sub", "row", None),
        P("sub", None, "row"),
        P("sub", None, "row"),
    ) + (P("sub", "row"),) * 9
    out_specs = (P("sub", None, "row"), P("sub", "row"))
    return jax.shard_map(
        functools.partial(on_device, subs, rows),
        mesh=mesh, in_specs=in_specs, out_specs=out_specs, check_vma=False,
    )
```

```python
import functools

import jax
import jax.numpy as jnp
from jax import lax
from jax.experimental import pallas as pl
from jax.experimental.pallas import tpu as pltpu
from jax.sharding import PartitionSpec as P

STEPS = 16
HISTORY = 32
NEWTON = 2
LANES = 128
TAGS = 3
HALVES = 2
PART = STEPS // 2

half_step = 0.25
knee_volts = 1.5
cubic_term = 0.25

F32 = jnp.float32
BF16 = jnp.bfloat16
MESH = pl.DeviceIdType.MESH
NN = (((1,), (0,)), ((), ()))
NT = (((1,), (1,)), ((), ()))
HIGHEST = lax.Precision.HIGHEST


def iota(shape, axis):
    return lax.broadcasted_iota(jnp.int32, shape, axis)


def hi_lo(x):
    high = x.astype(BF16)
    return high, (x - high.astype(F32)).astype(BF16)


def stack_hi_lo(x):
    return jnp.concatenate(hi_lo(x), axis=0)


def dot(a, b, dims=NN):
    return lax.dot_general(a, b, dims, preferred_element_type=F32)


def four_terms(r):
    n, m = r.shape[0] // 2, r.shape[1] // 2
    return (r[:n, :m] + r[n:, :m]) + (r[:n, m:] + r[n:, m:])


def kernel(
    subs, rows, ports, slice_len, arrests, cores, n_small,
    inv, src, *refs,
):
    small_hbm, refs = refs[:n_small], refs[n_small:]
    (
        out, hist, tags_i, gains, slots, m32, m2, mp2, gath, unit, got_units, elem, fst,
        x2, wc, fall, vo, cu, acc, hacc,
        small_sem, inv_sem, line_sem, line_recv, unit_sem, sub_sem, sub_in, both_sem, elem_sem, fst_sem,
    ) = refs
    s = lax.axis_index("sub")
    me = lax.axis_index("row")
    z, c = me // 2, me % 2
    zn = rows // 2
    partner = z * 2 + (1 - c)
    elems = arrests + cores
    group = LANES // elems
    total = rows * elems
    halves = total // LANES
    peers = subs - 1

    barrier = pltpu.get_barrier_semaphore()
    for j in range(1, rows):
        pl.semaphore_signal(barrier, inc=1, device_id=(s, lax.rem(me + j, rows)), device_id_type=MESH)
    bits = [1 << k for k in range((subs - 1).bit_length())]
    for bit in bits:
        pl.semaphore_signal(barrier, inc=1, device_id=(s ^ bit, me), device_id_type=MESH)

    ints, floats = small_hbm[1:4], small_hbm[4:8]
    pltpu.make_async_copy(small_hbm[0], hist, small_sem.at[0]).start()
    for i, ref in enumerate(ints):
        pltpu.make_async_copy(ref, tags_i.at[pl.ds(i, 1)], small_sem.at[1]).start()
    for i, ref in enumerate(floats):
        pltpu.make_async_copy(ref, gains.at[pl.ds(i, 1)], small_sem.at[2]).start()
    for i, ref in enumerate(small_hbm[8:]):
        pltpu.make_async_copy(ref, slots.at[i], small_sem.at[3]).start()
    src_copy = pltpu.make_async_copy(src.at[0], gath.at[me], small_sem.at[4])
    src_copy.start()

    def wait_all(ref, sem):
        pltpu.make_async_copy(ref, ref, sem).wait()

    wait_all(hist, small_sem.at[0])
    wait_all(tags_i.at[pl.ds(0, len(ints))], small_sem.at[1])
    wait_all(gains.at[pl.ds(0, len(floats))], small_sem.at[2])
    wait_all(slots, small_sem.at[3])
    dest, port, delay = (tags_i[i : i + 1, :] for i in range(len(ints)))
    prev, flux, again, cgain = (gains[i : i + 1, :] for i in range(len(floats)))

    span = m32.shape[1] // HALVES

    def inv_copy(h):
        cols = pl.ds(h * span, span)
        return pltpu.make_async_copy(inv.at[0, :, cols], m32.at[:, cols], inv_sem.at[h])

    for h in range(HALVES):
        inv_copy(h).start()

    shifted = hist[0]
    shift = HISTORY - delay
    bit = 1
    while bit <= HISTORY - STEPS:
        moved = pltpu.roll(shifted, HISTORY - bit, 0)
        shifted = jnp.where((shift // bit) % 2 == 1, moved, shifted)
        bit *= 2

    lane16a, row16a = iota((arrests, LANES), 1), iota((arrests, LANES), 0)
    lane16c, row16c = iota((cores, LANES), 1), iota((cores, LANES), 0)
    put_a = jnp.where(lane16a % elems == row16a, 1.0, 0.0).astype(BF16)
    put_c = jnp.where(lane16c % elems == row16c + arrests, 1.0, 0.0).astype(BF16)
    slot_a = jnp.broadcast_to(slots[0].astype(F32), (8, arrests)).astype(BF16)
    slot_c = jnp.broadcast_to(slots[1].astype(F32), (8, cores)).astype(BF16)
    slot_row = (dot(slot_a, put_a) + dot(slot_c, put_c))[0:1, :]
    hit = iota((ports, LANES), 0).astype(F32) == slot_row
    slot_tiled = jnp.where(hit, 1.0, 0.0)
    slot_own = jnp.where(iota((ports, LANES), 1) // elems == me % group, slot_tiled, 0.0)
    r8 = iota((8, ports), 0)
    params = jnp.where(
        r8 == TAGS,
        iota((8, ports), 1).astype(F32),
        jnp.where(
            r8 == TAGS + 1,
            again,
            jnp.where(r8 == TAGS + 2, cgain, jnp.where(r8 == TAGS + 3, prev, flux)),
        ),
    )
    p1 = params.astype(BF16).astype(F32)
    p2 = (params - p1).astype(BF16).astype(F32)
    parts = dot(jnp.concatenate([p1, p2, params - p1 - p2], axis=0).astype(BF16), slot_own.astype(BF16))
    par = (parts[:8] + parts[8:16]) + parts[16:24]
    k8 = iota((8, LANES), 0)
    tags = jnp.where(k8 == 0, dest, jnp.where(k8 == 1, port // ports, port % ports))
    mine_at = c * zn + z
    unit[mine_at, :STEPS, :] = shifted[:STEPS, :]
    unit[mine_at, STEPS:, :] = jnp.where(k8 < TAGS, tags.astype(F32), par)

    def remote(ref_from, ref_to, send, recv, to_sub, to_row):
        return pltpu.make_async_remote_copy(
            src_ref=ref_from, dst_ref=ref_to, send_sem=send, recv_sem=recv,
            device_id=(to_sub, to_row), device_id_type=MESH,
        )

    def unit_copy(zz, at, target):
        ref = unit.at[c * zn + zz]
        return remote(ref, ref, unit_sem.at[0], unit_sem.at[1 + at], s, target)

    def line_copy(b, target):
        return remote(gath.at[b], gath.at[b], line_sem.at[0], line_recv.at[b], s, target)

    def part_copy(h, b, target):
        ref = gath.at[b, pl.ds(h * PART, PART)]
        return remote(ref, ref, line_sem.at[0], line_recv.at[b if h == 0 else rows], s, target)

    def relay_copy(h, b, target):
        ref = gath.at[b, pl.ds(h * PART, PART)]
        return remote(ref, ref, line_sem.at[0], line_recv.at[b], s, target)

    def pass_copy(b):
        return remote(gath.at[b], gath.at[b], line_sem.at[1], line_recv.at[b], s, partner)

    def send_subs(zz):
        for j in range(1, subs):
            remote(
                unit.at[c * zn + zz], got_units.at[c, j - 1, zz], sub_sem.at[0], sub_sem.at[1], s ^ j, me
            ).start()

    def both_copy(cc):
        return remote(got_units.at[cc], got_units.at[cc], both_sem.at[0], both_sem.at[1], s, partner)

    def elem_copy(b, kind, target):
        return remote(elem.at[b], elem.at[b], elem_sem.at[0], elem_sem.at[1 + kind], s, target)

    def fst_copy(target):
        return remote(fst.at[me], fst.at[me], fst_sem.at[0], fst_sem.at[1], s, target)

    def sent(ref, sem):
        remote(ref, ref, sem, sem, s, partner).wait_send()

    def arrived(ref, sem):
        remote(ref, ref, sem, sem, s, partner).wait_recv()

    src_copy.wait()
    pl.semaphore_wait(barrier, rows - 1 + len(bits))

    def tell_subs(k):
        for bit in bits:
            pl.semaphore_signal(sub_in.at[k], inc=1, device_id=(s ^ bit, me), device_id_type=MESH)

    tell_subs(0)

    for j in range(1, zn):
        unit_copy(z, z, lax.rem(z + j, zn) * 2 + c).start()
    unit_copy(z, zn, partner).start()

    def send_near(target, relayed):
        @pl.when(relayed)
        def _():
            for h in range(2):
                part_copy(h, me, target).start()

        @pl.when(jnp.logical_not(relayed))
        def _():
            line_copy(me, target).start()

    for dist in [1] + list(range(zn - 1, 1, -1)):
        up, down = z + dist, z - dist

        @pl.when(jnp.logical_and(up < zn, jnp.logical_or(dist != 2, up != zn - 1)))
        def _():
            if dist == 1:
                send_near(up * 2 + c, up == zn - 2)
            else:
                line_copy(me, up * 2 + c).start()

        @pl.when(jnp.logical_and(down >= 0, jnp.logical_or(dist != 2, down != 0)))
        def _():
            if dist == 1:
                send_near(down * 2 + c, down == 1)
            else:
                line_copy(me, down * 2 + c).start()

    pass_copy(me).start()
    lower, upper = z == 1, z == zn - 2
    relays = jnp.logical_or(lower, upper)
    skips = jnp.logical_or(z == 2, z == zn - 3)
    znear = jnp.where(z < zn // 2, z + 1, z - 1)

    hacc[...] = jnp.zeros_like(hacc)

    def split_block(b, carry):
        cols = pl.ds(pl.multiple_of(b * slice_len, LANES), slice_len)
        high, low = hi_lo(m32[:, cols])
        m2[:ports, cols] = high
        m2[ports:, cols] = low
        at_ports = pl.ds(pl.multiple_of(b * ports, LANES), ports)
        mp2[:ports, at_ports] = high[:, :ports]
        mp2[ports:, at_ports] = low[:, :ports]
        return carry

    def columns(b, count):
        return pl.ds(pl.multiple_of(b * slice_len, LANES), count * slice_len)

    def chip_term(zb):
        both = jnp.concatenate([gath[zb * 2], gath[zb * 2 + 1]], axis=1)
        return dot(stack_hi_lo(both), m2[:, columns(zb * 2, 2)], NT)

    def use_sources(b):
        acc[...] += dot(stack_hi_lo(gath[b]), m2[:, columns(b, 1)], NT)

    for h in range(HALVES):
        inv_copy(h).wait()
        lax.fori_loop(h * rows // HALVES, (h + 1) * rows // HALVES, split_block, 0)
    pass_copy(partner).wait_recv()
    acc[...] = chip_term(z)

    for k in range(len(bits) - 1):
        pl.semaphore_wait(sub_in.at[k], len(bits))
        if k < len(bits) - 2:
            tell_subs(k + 1)
    send_subs(z)
    toward = jnp.where(z < zn // 2, 1, zn - 1)
    for j in range(1, zn):
        zz = lax.rem(z + j * toward, zn)
        unit_copy(zz, zz, partner).wait_recv()
        unit_copy(zz, zn, partner).start()
        send_subs(zz)

    low_z = jnp.minimum(z, zn - 1 - z)
    one = jnp.minimum(z + 1, 1)

    def other_chips(lo, hi, act):
        def body(q, carry):
            inside = jnp.where(q < low_z, low_z - 1 - q, q + 2)
            zb = jnp.where(low_z == 0, zn - 1 - q, inside)
            act(jnp.where(z < zn // 2, zb, zn - 1 - zb))
            return carry

        lax.fori_loop(lo, hi - 1 + one, body, 0)

    def take(zb):
        line_copy(zb * 2 + c, partner).wait_recv()
        pass_copy(zb * 2 + c).start()

    def use_own(zb):
        use_sources(zb * 2 + c)

    def use_passed(zb):
        pass_copy(zb * 2 + 1 - c).wait_recv()
        use_sources(zb * 2 + 1 - c)

    near = znear * 2 + c
    outer = jnp.where(lower, z - 1, z + 1) * 2 + 1

    @pl.when(relays)
    def _():
        for h in range(2):
            part_copy(h, near, partner).wait_recv()
            relay_copy(h, near, outer).start()

    @pl.when(jnp.logical_not(relays))
    def _():
        line_copy(near, partner).wait_recv()

    pass_copy(znear * 2 + c).start()
    use_own(znear)
    use_passed(znear)

    arrived(unit.at[pl.ds(0, zn)], unit_sem.at[1 + zn])
    all_par = jnp.concatenate(
        [
            sum(unit[(h * group + i) % 2 * zn + (h * group + i) // 2, STEPS:, :] for i in range(group))
            for h in range(halves)
        ],
        axis=1,
    )
    slots_all = all_par[TAGS : TAGS + 1, :]
    at_slot = iota((ports, total), 0).astype(F32) == slots_all
    owner_of = iota((ports, total), 1) // elems
    choose = [
        jnp.where(jnp.logical_and(at_slot, owner_of == r), 1.0, 0.0).astype(BF16) for r in range(rows)
    ]
    x2[...] = dot(mp2[...], jnp.concatenate(choose, axis=0)).astype(BF16)
    slot_cols = jnp.transpose(slot_tiled)[:elems].astype(BF16)
    elem[me] = dot(slot_cols, x2[:ports, :]) + dot(slot_cols, x2[ports:, :])
    for j in range(1, zn):
        elem_copy(me, 0, lax.rem(z + j, zn) * 2 + c).start()
    elem_copy(me, 1, partner).start()

    def take_use(zb):
        take(zb)

        @pl.when(c == 1)
        def _():
            use_own(zb)

    other_chips(0, 1, take_use)
    arrived(got_units.at[c], sub_sem.at[1])
    both_copy(c).start()

    def use_records(cc):
        blocks = [(x, zz) for zz in range(zn) for x in range(peers)]
        values = jnp.concatenate([got_units[cc, x, zz, :STEPS, :] for x, zz in blocks], axis=1)
        tag = jnp.concatenate([got_units[cc, x, zz, STEPS:, :] for x, zz in blocks], axis=1)
        owner = jnp.where(tag[0:1, :] == s.astype(F32), tag[1:2, :], -1.0)
        spot = tag[2:3, :]
        wide = values.shape[1]
        land = jnp.where(iota((ports, wide), 0).astype(F32) == spot, 1.0, 0.0).astype(BF16)
        high, low = hi_lo(values)
        wide_owner = jnp.broadcast_to(owner, (STEPS, wide))
        split = []
        for r in range(rows):
            mine = jnp.where(wide_owner == float(r), 1.0, 0.0).astype(BF16)
            split += [high * mine, low * mine]
        hacc[...] += dot(jnp.concatenate(split, axis=0), land, NT)

    use_records(c)
    at_end = jnp.logical_or(z == 0, z == zn - 1)

    def relayed_chip(zb):
        return jnp.logical_and(at_end, jnp.abs(z - zb) == 2)

    def last_take(zb):
        @pl.when(jnp.logical_and(relayed_chip(zb), c == 1))
        def _():
            for p in (1, 0):
                line_copy(zb * 2 + p, partner).wait_recv()
                pass_copy(zb * 2 + p).start()

        @pl.when(jnp.logical_not(relayed_chip(zb)))
        def _():
            take(zb)

    def first_chip(zb):
        pass_copy(zb * 2 + 1).wait_recv()
        acc[...] += chip_term(zb)

    def last_chip(zb):
        @pl.when(jnp.logical_and(relayed_chip(zb), c == 0))
        def _():
            pass_copy(zb * 2).wait_recv()

        @pl.when(jnp.logical_not(jnp.logical_and(relayed_chip(zb), c == 1)))
        def _():
            pass_copy(zb * 2 + 1 - c).wait_recv()

        acc[...] += chip_term(zb)

    @pl.when(c == 0)
    def _():
        other_chips(0, 1, first_chip)

    other_chips(1, zn - 2, last_take)

    @pl.when(c == 1)
    def _():
        other_chips(0, 1, use_passed)

    both_copy(1 - c).wait_recv()
    use_records(1 - c)
    other_chips(1, zn - 2, last_chip)

    landed = jnp.concatenate(
        [
            hacc[2 * r * STEPS : (2 * r + 1) * STEPS, :] + hacc[(2 * r + 1) * STEPS : (2 * r + 2) * STEPS, :]
            for r in range(rows)
        ],
        axis=1,
    )
    first = four_terms(acc[...] - dot(stack_hi_lo(landed), mp2[...], NT))
    mine = dot(stack_hi_lo(first), slot_own.astype(BF16))
    fst[me] = mine[:STEPS] + mine[STEPS:]
    for j in range(1, rows):
        fst_copy(lax.rem(me + j, rows)).start()

    arrived(elem.at[pl.ds(0, zn - 1)], elem_sem.at[1])
    for j in range(1, zn):
        elem_copy(lax.rem(z + j, zn) * 2 + c, 1, partner).start()
    arrived(elem.at[pl.ds(0, zn)], elem_sem.at[2])

    w = elem[...].reshape(total, total)
    self_row = jnp.sum(jnp.where(iota((total, total), 0) == iota((total, total), 1), w, 0.0), axis=0, keepdims=True)
    w_hi, w_lo = hi_lo(jnp.transpose(w))
    wc[:, :total] = w_hi
    wc[:, total:] = w_lo

    full = (8, total)
    is_arrest = iota(full, 1) % elems < arrests
    rowp = lambda i: jnp.broadcast_to(all_par[TAGS + i : TAGS + i + 1, :], full)
    arrest_gain = jnp.where(is_arrest, rowp(1), 0.0)
    core_gain = jnp.where(is_arrest, 0.0, rowp(2))
    elem_self = jnp.broadcast_to(self_row, full)
    volts0 = rowp(3)
    flux0 = rowp(4)
    put = jnp.where(jnp.logical_and(at_slot, owner_of == me), 1.0, 0.0).astype(BF16)
    here = dot(jnp.ones((8, total), BF16), put, NT)[0:1]

    sent(got_units.at[c], sub_sem.at[0])
    sent(got_units.at[c], both_sem.at[0])
    passes = zn + at_end.astype(jnp.int32) * (2 * c - 1)
    for n in range(zn - 1, zn + 2):
        @pl.when(passes == n)
        def _():
            sent(gath.at[pl.ds(0, n)], line_sem.at[1])

    line_sends = zn - 1 + relays.astype(jnp.int32) - skips.astype(jnp.int32)
    for n in range(zn - 2, zn + 1):
        @pl.when(line_sends == n)
        def _():
            sent(gath.at[pl.ds(0, n)], line_sem.at[0])

    sent(unit.at[pl.ds(0, 2 * zn - 1)], unit_sem.at[0])
    sent(elem.at[pl.ds(0, 2 * zn - 1)], elem_sem.at[0])
    arrived(fst.at[pl.ds(0, rows - 1)], fst_sem.at[1])
    fall[...] = jnp.concatenate(
        [sum(fst[h * group + i] for i in range(group)) for h in range(halves)], axis=1
    )

    def advance(t, carry):
        voltage, flux_now = carry
        first_now = jnp.broadcast_to(fall[pl.ds(t, 1), :], full)
        iterate = voltage
        for newton_pass in range(NEWTON):
            linked = flux_now + half_step * (iterate + voltage)
            ratio = iterate * (1.0 / knee_volts)
            rr = ratio * ratio
            ll = linked * linked
            current = arrest_gain * (iterate * (1.0 + rr)) + core_gain * (linked * (1.0 + cubic_term * ll))
            slope = arrest_gain * (1.0 + 3.0 * rr) + core_gain * (half_step + (half_step * 3.0 * cubic_term) * ll)
            recip = 1.0 / (1.0 + elem_self * slope)
            got = dot(stack_hi_lo(current), wc[...])
            settled = iterate - (iterate - first_now) * recip
            coupled = (got[:8, :total] + got[8:, :total]) + got[:8, total:]
            iterate = settled - coupled * recip
        vo[pl.ds(t, 1), :] = iterate[0:1]
        cu[pl.ds(t, 1), :] = current[0:1]
        return iterate, flux_now + half_step * (iterate + voltage)

    lax.fori_loop(0, STEPS, advance, (volts0, flux0), unroll=8)

    reach = four_terms(dot(stack_hi_lo(cu[...]), x2[...], NT))
    placed = dot(stack_hi_lo(vo[...]), put, NT)
    stacked = jnp.where(here > 0.5, placed[:STEPS] + placed[STEPS:], first - reach)
    out[:STEPS, :] = stacked
    summed = jnp.sum(stacked, axis=0, keepdims=True)
    last_flux = flux + half_step * (prev + 2.0 * summed - stacked[STEPS - 1 : STEPS])
    out[STEPS:, :] = jnp.broadcast_to(last_flux, (8, ports))
    sent(fst.at[pl.ds(0, rows - 1)], fst_sem.at[0])


def give(both, volts, last_flux):
    volts[0] = both[:STEPS, :]
    last_flux[...] = both[STEPS : STEPS + 1, :]


def on_device(subs, rows, *args):
    inverse, sources = args[0], args[1]
    ports = inverse.shape[1]
    order = inverse.shape[2]
    slice_len = sources.shape[2]
    arrests, cores = args[10].shape[1], args[11].shape[1]
    elems = arrests + cores
    total = rows * elems
    zn = rows // 2
    vmem = pl.BlockSpec(memory_space=pltpu.VMEM)
    hbm = pl.BlockSpec(memory_space=pl.ANY)
    dma = pltpu.SemaphoreType.DMA
    small = args[2:]
    both = pl.pallas_call(
        functools.partial(kernel, subs, rows, ports, slice_len, arrests, cores, len(small)),
        out_shape=pltpu.VMEM((STEPS + 8, ports), F32),
        in_specs=[hbm] * len(args),
        out_specs=vmem,
        scratch_shapes=[
            pltpu.VMEM(small[0].shape, F32),
            pltpu.VMEM((8, LANES), jnp.int32),
            pltpu.VMEM((8, LANES), F32),
            pltpu.VMEM((2, 1, arrests), jnp.int32),
            pltpu.VMEM((ports, order), F32),
            pltpu.VMEM((2 * ports, order), BF16),
            pltpu.VMEM((2 * ports, rows * ports), BF16),
            pltpu.VMEM((rows, STEPS, slice_len), F32),
            pltpu.VMEM((2 * zn, STEPS + 8, LANES), F32),
            pltpu.VMEM((2, subs - 1, zn, STEPS + 8, LANES), F32),
            pltpu.VMEM((rows, elems, total), F32),
            pltpu.VMEM((rows, STEPS, LANES), F32),
            pltpu.VMEM((2 * ports, total), BF16),
            pltpu.VMEM((total, 2 * total), BF16),
            pltpu.VMEM((STEPS, total), F32),
            pltpu.VMEM((STEPS, total), F32),
            pltpu.VMEM((STEPS, total), F32),
            pltpu.VMEM((2 * STEPS, 2 * ports), F32),
            pltpu.VMEM((2 * STEPS * rows, ports), F32),
            dma((5,)),
            dma((HALVES,)),
            dma((2,)),
            dma((rows + 1,)),
            dma((zn + 2,)),
            dma((2,)),
            pltpu.SemaphoreType.REGULAR((max((subs - 1).bit_length() - 1, 1),)),
            dma((2,)),
            dma((3,)),
            dma((2,)),
        ],
        compiler_params=pltpu.CompilerParams(collective_id=0, has_side_effects=True),
        name="window",
    )(*args)
    return pl.pallas_call(
        give,
        out_shape=(
            jax.ShapeDtypeStruct((1, STEPS, ports), F32),
            jax.ShapeDtypeStruct((1, ports), F32),
        ),
        in_specs=[vmem],
        out_specs=(vmem, vmem),
        name="give",
    )(pltpu.with_memory_space_constraint(both, pltpu.VMEM))


def solution(mesh):
    subs, rows = mesh.shape["sub"], mesh.shape["row"]
    in_specs = (
        P("sub", "row", None),
        P("sub", None, "row"),
        P("sub", None, "row"),
    ) + (P("sub", "row"),) * 9
    out_specs = (P("sub", None, "row"), P("sub", "row"))
    return jax.shard_map(
        functools.partial(on_device, subs, rows),
        mesh=mesh, in_specs=in_specs, out_specs=out_specs, check_vma=False,
    )
```
